32 devices in a mesh: dp: 8 (over y, x, core), fsdp: 4 (over z).
Axes of the slice: x: 2, y: 2, z: 4, core: 2. Of those that a mesh axis runs over, the one named last changes fastest.
Arguments:
- inputs: bfloat16 [12288, 1024], P(('dp', 'fsdp')), may hold values from -6 to 6
- cotangent: bfloat16 [12288, 1024], P(('dp', 'fsdp')), may hold values from -6 to 6
- lengths: int32 [64, 3], P(('dp', 'fsdp')), may hold values from 0 to 192, as said below
- buckets: int32 [64], P(('dp', 'fsdp')), may hold values from 0 to 2, as said below
- ffn1_in: bfloat16 [1024, 4096], P('fsdp'), may hold values from -0.1875 to 0.1875
- ffn1_out: bfloat16 [4096, 1024], P('fsdp'), may hold values from -0.09375 to 0.09375
- attn_in: bfloat16 [1024, 4096], P('fsdp'), may hold values from -0.1875 to 0.1875
- attn_out: bfloat16 [1024, 1024], P('fsdp'), may hold values from -0.5 to 0.5
- conv_in: bfloat16 [1024, 2048], P('fsdp'), may hold values from -0.1875 to 0.1875
- conv_out: bfloat16 [1024, 1024], P('fsdp'), may hold values from -0.1875 to 0.1875
- ffn2_in: bfloat16 [1024, 4096], P('fsdp'), may hold values from -0.1875 to 0.1875
- ffn2_out: bfloat16 [4096, 1024], P('fsdp'), may hold values from -0.09375 to 0.09375
- norm_gains: bfloat16 [6, 1024], P(None, 'fsdp'), may hold values from 0.5 to 1.5
- pos_bias: bfloat16 [2, 1024], P(None, 'fsdp'), may hold values from -6 to 6
- kernel: bfloat16 [5, 1024], P(None, 'fsdp'), may hold values from -2.5 to 2.5
Outputs:
- outputs: bfloat16 [12288, 1024], P(('dp', 'fsdp'))
- grad_inputs: float32 [12288, 1024], P(('dp', 'fsdp'))
- grad_ffn1_in: float32 [1024, 4096], P('fsdp')
- grad_ffn1_out: float32 [4096, 1024], P('fsdp')
- grad_attn_in: float32 [1024, 4096], P('fsdp')
- grad_attn_out: float32 [1024, 1024], P('fsdp')
- grad_conv_in: float32 [1024, 2048], P('fsdp')
- grad_conv_out: float32 [1024, 1024], P('fsdp')
- grad_ffn2_in: float32 [1024, 4096], P('fsdp')
- grad_ffn2_out: float32 [4096, 1024], P('fsdp')
- grad_norm_gains: float32 [6, 1024], P(None, 'fsdp')
- grad_pos_bias: float32 [2, 1024], P(None, 'fsdp')
- grad_kernel: float32 [5, 1024], P(None, 'fsdp')
The draws below stay inside these ranges and needn't reach their ends.
Inputs may be any that keep to these rules, and one draw needn't show every extreme that they name: `buckets`: bucket id of each micro-batch; its bucket holds 64 * (id + 1) frames; micro-batch 0 has id 2. lengths[m, s] is the frame count of slot s of micro-batch m: slot s holds an utterance when s < 192 // (64 * (id + 1)), of a quarter of the bucket to the whole bucket, slot 0 exactly the whole bucket; other slots hold 0.
All inputs are finite; a program needn't handle non-finite values.
Results may differ from the reference program's by a relative error of at most 0.023.
Values may be sent and summed in bfloat16 or wider, within the bound.
A program may use at most 256 MiB of HBM per device.

```python
import math
import jax
import jax.numpy as jnp
from jax import lax

D = 1024
FF = 4096
HEADS = 8
HEAD_DIM = 128
KERNEL = 5
BUCKET = 64
MICRO = 2
FRAMES = 192
SLOTS = 3
TOKENS = 12288
DEVICES = 32


def draw_plan(key):
    batch_count = MICRO * DEVICES
    bucket_ids = jax.random.randint(jax.random.fold_in(key, 11), (batch_count,), 0, 3)
    bucket_ids = jnp.where(jnp.arange(batch_count) == 0, 2, bucket_ids).astype(jnp.int32)
    bucket_len = BUCKET * (bucket_ids + 1)
    raw_bits = jax.random.randint(jax.random.fold_in(key, 12), (batch_count, SLOTS), 0, 1 << 20)
    least_len = bucket_len // 4
    length_table = least_len[:, None] + raw_bits % (bucket_len - least_len + 1)[:, None]
    slot_index = jnp.arange(SLOTS)
    length_table = jnp.where(slot_index[None, :] == 0, bucket_len[:, None], length_table)
    in_use = slot_index[None, :] < (FRAMES // bucket_len)[:, None]
    return (bucket_ids, jnp.where(in_use, length_table, 0).astype(jnp.int32))


def draw_lengths(key, part):
    return draw_plan(key)[1]


def draw_buckets(key, part):
    return draw_plan(key)[0]


def levels(rng, dims, split, low, top_value):
    def one(dim, parts):
        draws = jax.random.uniform(jax.random.fold_in(jax.random.fold_in(rng, 6), dim), (parts,), jnp.float32, low / len(split), top_value / len(split))
        return jnp.repeat(jnp.exp(draws), dims[dim] // parts).reshape((-1,) + (1,) * (len(dims) - dim - 1))

    gain = one(*split[0])
    for cut in split[1:]:
        gain = gain * one(*cut)
    return gain


def gaussian(stream_key, dims, width, limit, split=(), held_as=jnp.bfloat16):
    loudness = levels(stream_key, dims, split, -0.22, 0.18) if split else 1.0
    drawn = jax.random.normal(stream_key, dims, jnp.float32) * width * loudness
    return jnp.minimum(jnp.maximum(drawn, -limit), limit).astype(held_as)


def setup_inputs(seed: int = 0) -> dict:
    arg_keys = jax.random.split(jax.random.key(seed), 16)
    inputs = gaussian(arg_keys[0], (TOKENS, D), 1.0, 6.0, ((0, 32),))
    cotangent = gaussian(arg_keys[1], (TOKENS, D), 1.0, 6.0, ((0, 32),))
    lengths = draw_lengths(jax.random.fold_in(arg_keys[15], 71), 0)
    buckets = draw_buckets(jax.random.fold_in(arg_keys[15], 71), 0)
    ffn1_in = gaussian(arg_keys[4], (D, FF), D ** -0.5, 0.1875, ((0, 4),))
    ffn1_out = gaussian(arg_keys[5], (FF, D), FF ** -0.5, 0.09375, ((0, 4),))
    attn_in = gaussian(arg_keys[6], (D, 4 * D), D ** -0.5, 0.1875, ((0, 4),))
    attn_out = gaussian(arg_keys[7], (D, D), (D // 8) ** -0.5, 0.5, ((0, 4),))
    conv_in = gaussian(arg_keys[8], (D, 2 * D), D ** -0.5, 0.1875, ((0, 4),))
    conv_out = gaussian(arg_keys[9], (D, D), D ** -0.5, 0.1875, ((0, 4),))
    ffn2_in = gaussian(arg_keys[10], (D, FF), D ** -0.5, 0.1875, ((0, 4),))
    ffn2_out = gaussian(arg_keys[11], (FF, D), FF ** -0.5, 0.09375, ((0, 4),))
    norm_gains = jnp.clip(1.0 + 0.1 * jax.random.normal(arg_keys[12], (6, D), jnp.float32), 0.5, 1.5).astype(jnp.bfloat16)
    pos_bias = gaussian(arg_keys[13], (2, D), 1.0, 6.0, ((1, 4),))
    kernel = gaussian(arg_keys[14], (KERNEL, D), KERNEL ** -0.5, 2.5, ((1, 4),))
    return dict(inputs=inputs, cotangent=cotangent, lengths=lengths, buckets=buckets, ffn1_in=ffn1_in, ffn1_out=ffn1_out, attn_in=attn_in, attn_out=attn_out, conv_in=conv_in, conv_out=conv_out, ffn2_in=ffn2_in, ffn2_out=ffn2_out, norm_gains=norm_gains, pos_bias=pos_bias, kernel=kernel)


@jax.custom_vjp
def low(v):
    return lax.optimization_barrier(v.astype(jnp.bfloat16)).astype(jnp.float32)

@jax.custom_vjp
def low_back(v):
    return v

def low_keep(v):
    return (low(v), None)

def low_pass(kept, grad):
    return (grad,)

def back_keep(v):
    return (v, None)

def back_low(kept, grad):
    return (low(grad),)
low.defvjp(low_keep, low_pass)
low_back.defvjp(back_keep, back_low)

def product(left_side, right_side):
    return jnp.dot(left_side, right_side, precision=lax.Precision.HIGHEST, preferred_element_type=jnp.float32)

def layer_norm(values, gain_row):
    centred = values - lax.optimization_barrier(jnp.mean(values, axis=-1, keepdims=True))
    spread = lax.optimization_barrier(jnp.mean(centred * centred, axis=-1, keepdims=True))
    return centred * lax.rsqrt(spread + 1e-05) * gain_row

def swish_act(values):
    return values * jax.nn.sigmoid(values)

def neighbour(values, offset):
    if offset > 0:
        filler = jnp.zeros((offset,) + values.shape[1:], values.dtype)
        return jnp.concatenate([values[offset:], filler], axis=0)
    if offset < 0:
        filler = jnp.zeros((-offset,) + values.shape[1:], values.dtype)
        return jnp.concatenate([filler, values[:offset]], axis=0)
    return values

def frame_plan(utter_len, bucket_id):
    position = jnp.arange(FRAMES, dtype=jnp.int32)
    bucket_len = BUCKET * (bucket_id + 1)
    segment = position // bucket_len
    offset_in = position - segment * bucket_len
    slot_index = jnp.arange(SLOTS, dtype=jnp.int32)
    slot_limit = lax.optimization_barrier(jnp.sum(jnp.where(segment[:, None] == slot_index[None, :], utter_len[None, :], 0), axis=1))
    is_valid = offset_in < slot_limit
    allowed = (segment[:, None] == segment[None, :]) & is_valid[None, :] | (position[:, None] == position[None, :])
    tap_list = []
    for tap_index in range(KERNEL):
        shift_by = tap_index - KERNEL // 2
        same_slot = (neighbour(segment + 1, shift_by) == segment + 1) & neighbour(is_valid, shift_by)
        tap_list.append(same_slot.astype(jnp.float32))
    return (allowed, jnp.stack(tap_list, axis=0))

def sinusoid():
    distance = (jnp.arange(2 * FRAMES - 1, dtype=jnp.int32) - (FRAMES - 1)).astype(jnp.float32)
    freq_index = jnp.arange(D // 2, dtype=jnp.int32).astype(jnp.float32)
    freq_rates = jnp.exp(freq_index * (-2.0 * math.log(10000.0) / D))
    angles = distance[:, None] * freq_rates[None, :]
    return jnp.stack([jnp.sin(angles), jnp.cos(angles)], axis=-1).reshape(2 * FRAMES - 1, D)

def skew_rows(pos_table):
    head_count, row_count, col_width = pos_table.shape
    padded = jnp.pad(pos_table, ((0, 0), (0, 0), (0, row_count)))
    flat_view = padded.reshape(head_count, row_count * (col_width + row_count))[:, :row_count * (col_width + row_count - 1)]
    return flat_view.reshape(head_count, row_count, col_width + row_count - 1)

def relative_scores(pos_table):
    row_count = pos_table.shape[1]
    return skew_rows(pos_table)[:, :, row_count - 1:2 * row_count - 1]

def depthwise(values, kernel_rows, tap_masks):
    running = jnp.zeros_like(values)
    for tap_index in range(KERNEL):
        moved = neighbour(values, tap_index - KERNEL // 2)
        running = running + moved * tap_masks[tap_index][:, None] * kernel_rows[tap_index][None, :]
    return running

def feed_forward(values, gain_row, weight_in, weight_out):
    normed = low(layer_norm(values, gain_row))
    hidden = low_back(product(normed, weight_in))
    active = low(swish_act(hidden))
    return low_back(product(active, weight_out))

def self_attention(values, gain_row, weight_qkv, weight_out, bias_u, bias_v, positions, allowed):
    score_scale = HEAD_DIM ** (-0.5)
    normed = low(layer_norm(values, gain_row))
    project = low(low_back(product(normed, weight_qkv)))
    query_raw = project[:, :D]
    keys_h = project[:, D:2 * D].reshape(FRAMES, HEADS, HEAD_DIM)
    values_h = project[:, 2 * D:].reshape(FRAMES, HEADS, HEAD_DIM)
    query_u = low((query_raw + bias_u) * score_scale).reshape(FRAMES, HEADS, HEAD_DIM)
    query_v = low((query_raw + bias_v) * score_scale).reshape(FRAMES, HEADS, HEAD_DIM)
    content = jnp.einsum('ihd,jhd->hij', query_u, keys_h, precision=lax.Precision.HIGHEST)
    pos_heads = positions.reshape(2 * FRAMES - 1, HEADS, HEAD_DIM)
    pos_table = jnp.einsum('ihd,rhd->hir', query_v, pos_heads, precision=lax.Precision.HIGHEST)
    scores = low_back(content + relative_scores(pos_table))
    scores = jnp.where(allowed[None], scores, -1e+30)
    weights_low = low(jax.nn.softmax(scores, axis=-1))
    mixed_heads = jnp.einsum('hij,jhd->ihd', weights_low, values_h, precision=lax.Precision.HIGHEST)
    mixed_heads = low(low_back(mixed_heads.reshape(FRAMES, D)))
    return low_back(product(mixed_heads, weight_out))

def conv_module(values, gain_row, gain_inner, weight_in, weight_out, kernel_rows, tap_masks):
    normed = low(layer_norm(values, gain_row))
    gated = low_back(product(normed, weight_in))
    gated_out = gated[:, :D] * jax.nn.sigmoid(gated[:, D:])
    depth_out = depthwise(gated_out, kernel_rows, tap_masks)
    active = low(swish_act(layer_norm(depth_out, gain_inner)))
    return low_back(product(active, weight_out))

def one_batch(frames_block, utter_len, bucket_id, params, positions):
    ffn1_in, ffn1_out, attn_in, attn_out, conv_in, conv_out, ffn2_in, ffn2_out, gain_rows, pos_bias, kernel = params
    allowed, tap_masks = frame_plan(utter_len, bucket_id)
    section_one = frames_block + 0.5 * feed_forward(frames_block, gain_rows[0], ffn1_in, ffn1_out)
    section_two = section_one + self_attention(section_one, gain_rows[1], attn_in[:, :3 * D], attn_out, pos_bias[0], pos_bias[1], positions, allowed)
    section_three = section_two + conv_module(section_two, gain_rows[2], gain_rows[3], conv_in, conv_out, kernel, tap_masks)
    section_four = section_three + 0.5 * feed_forward(section_three, gain_rows[4], ffn2_in, ffn2_out)
    return layer_norm(section_four, gain_rows[5])

def reference(inputs, cotangent, lengths, buckets, ffn1_in, ffn1_out, attn_in, attn_out, conv_in, conv_out, ffn2_in, ffn2_out, norm_gains, pos_bias, kernel):
    params = tuple((weight_item.astype(jnp.float32) for weight_item in (ffn1_in, ffn1_out, attn_in, attn_out, conv_in, conv_out, ffn2_in, ffn2_out, norm_gains, pos_bias, kernel)))
    frames_all = inputs.astype(jnp.float32).reshape(-1, FRAMES, D)
    pos_source = sinusoid()

    def forward(frames_all, params):
        positions = low(low_back(product(low(pos_source), params[2][:, 3 * D:])))

        def run_batch(packed):
            return one_batch(packed[0], packed[1], packed[2], params, positions)
        return lax.map(jax.checkpoint(run_batch), (frames_all, lengths, buckets))
    result, pull_back = jax.vjp(forward, frames_all, params)
    grad_frames, grad_params = pull_back(cotangent.astype(jnp.float32).reshape(result.shape))
    return (result.reshape(-1, D).astype(jnp.bfloat16), grad_frames.reshape(-1, D), grad_params[0], grad_params[1], grad_params[2], grad_params[3], grad_params[4], grad_params[5], grad_params[6], grad_params[7], grad_params[8], grad_params[9], grad_params[10])
```

```python
from functools import partial
import math

import jax
import jax.numpy as jnp
from jax import lax
from jax.experimental import pallas as pl
from jax.experimental.pallas import tpu as pltpu
from jax.sharding import PartitionSpec as P

MESH = pl.DeviceIdType.MESH

D = 1024
HEADS = 8
HEAD_DIM = 128
KERNEL = 5
BUCKET = 64
MICRO = 2
FRAMES = 192
SLOTS = 3


def matmul(left_side, right_side):
    return jnp.dot(left_side, right_side, preferred_element_type=jnp.float32)


def left_product(left_side, right_side):
    return lax.dot_general(
        left_side, right_side, (((0,), (0,)), ((), ())), preferred_element_type=jnp.float32
    )


def right_product(left_side, right_side):
    return lax.dot_general(
        left_side, right_side, (((1,), (1,)), ((), ())), preferred_element_type=jnp.float32
    )


def layer_norm(values, gain_row):
    centred = values - jnp.mean(values, axis=-1, keepdims=True)
    spread = jnp.mean(centred * centred, axis=-1, keepdims=True)
    return centred * lax.rsqrt(spread + 1e-05) * gain_row


def swish_act(values):
    return values * jax.nn.sigmoid(values)


def neighbour(values, offset):
    if offset > 0:
        filler = jnp.zeros((offset,) + values.shape[1:], values.dtype)
        return jnp.concatenate([values[offset:], filler], axis=0)
    if offset < 0:
        filler = jnp.zeros((-offset,) + values.shape[1:], values.dtype)
        return jnp.concatenate([filler, values[:offset]], axis=0)
    return values


def frame_plan(utter_len, bucket_id):
    position = jnp.arange(FRAMES, dtype=jnp.int32)
    bucket_len = BUCKET * (bucket_id + 1)
    segment = position // bucket_len
    offset_in = position - segment * bucket_len
    slot_index = jnp.arange(SLOTS, dtype=jnp.int32)
    slot_limit = jnp.sum(
        jnp.where(segment[:, None] == slot_index[None, :], utter_len[None, :], 0), axis=1
    )
    is_valid = offset_in < slot_limit
    allowed = (segment[:, None] == segment[None, :]) & is_valid[None, :] | (
        position[:, None] == position[None, :]
    )
    tap_list = []
    for tap_index in range(KERNEL):
        shift_by = tap_index - KERNEL // 2
        same_slot = (neighbour(segment + 1, shift_by) == segment + 1) & neighbour(
            is_valid, shift_by
        )
        tap_list.append(same_slot.astype(jnp.float32))
    return (allowed, jnp.stack(tap_list, axis=0))


def sinusoid():
    distance = (jnp.arange(2 * FRAMES - 1, dtype=jnp.int32) - (FRAMES - 1)).astype(jnp.float32)
    freq_index = jnp.arange(D // 2, dtype=jnp.int32).astype(jnp.float32)
    freq_rates = jnp.exp(freq_index * (-2.0 * math.log(10000.0) / D))
    angles = distance[:, None] * freq_rates[None, :]
    return jnp.stack([jnp.sin(angles), jnp.cos(angles)], axis=-1).reshape(2 * FRAMES - 1, D)


def skew_rows(pos_table):
    head_count, row_count, col_width = pos_table.shape
    padded = jnp.pad(pos_table, ((0, 0), (0, 0), (0, row_count)))
    flat_view = padded.reshape(head_count, row_count * (col_width + row_count))[
        :, : row_count * (col_width + row_count - 1)
    ]
    return flat_view.reshape(head_count, row_count, col_width + row_count - 1)


def relative_scores(pos_table):
    row_count = pos_table.shape[2]
    flat = pos_table.reshape((-1,) + pos_table.shape[2:])
    moved = skew_rows(flat)[:, :, row_count - 1 : 2 * row_count - 1]
    return moved.reshape(pos_table.shape[:2] + moved.shape[1:])


def unskew_rows(grad_scores):
    head_count = grad_scores.shape[0]
    row_count = grad_scores.shape[1]
    wide_view = jnp.pad(grad_scores, ((0, 0), (0, 0), (row_count - 1, row_count - 1)))
    col_width = 3 * row_count - 2
    flat_view = jnp.pad(
        wide_view.reshape(head_count, row_count * col_width), ((0, 0), (0, row_count))
    )
    return flat_view.reshape(head_count, row_count, col_width + 1)[:, :, : 2 * row_count - 1]


def depthwise(values, kernel_rows, tap_masks):
    running = jnp.zeros_like(values)
    for tap_index in range(KERNEL):
        moved = neighbour(values, tap_index - KERNEL // 2)
        running = running + moved * tap_masks[tap_index][:, None] * kernel_rows[tap_index][None, :]
    return running


def conv_inner(gated, gain_inner, kernel_rows, tap_masks):
    gated_out = gated[:, :D] * jax.nn.sigmoid(gated[:, D:])
    return swish_act(layer_norm(depthwise(gated_out, kernel_rows, tap_masks), gain_inner))


def attn_scores(query_u, query_v, keys_h, positions, allowed):
    content = jnp.einsum("bihd,bjhd->bhij", query_u, keys_h, preferred_element_type=jnp.float32)
    pos_table = jnp.einsum("bihd,rhd->bhir", query_v, positions, preferred_element_type=jnp.float32)
    return jnp.where(allowed[:, None], content + relative_scores(pos_table), -1e30)


def ffn_forward(values, gain_row, weight_in, weight_out):
    normed, norm_pull = jax.vjp(layer_norm, values, gain_row)
    normed_low = normed.astype(jnp.bfloat16)
    hidden = matmul(normed_low, weight_in)
    active = swish_act(hidden).astype(jnp.bfloat16)
    return (matmul(active, weight_out), (norm_pull, normed_low, hidden, active))


def ffn_backward(grad_branch, kept_state, weight_in, weight_out):
    norm_pull, normed_low, hidden, active = kept_state
    grad_out = grad_branch.astype(jnp.bfloat16)
    weight_out_grad = left_product(active, grad_out)
    grad_active = right_product(grad_out, weight_out)
    swish_value, swish_pull = jax.vjp(swish_act, hidden)
    grad_hidden = swish_pull(grad_active)[0].astype(jnp.bfloat16)
    weight_in_grad = left_product(normed_low, grad_hidden)
    grad_normed = right_product(grad_hidden, weight_in)
    grad_values, grad_gain = norm_pull(grad_normed)
    return (grad_values, grad_gain[None], weight_in_grad, weight_out_grad)


def attn_forward(values, gain_row, weight_qkv, weight_out, bias_u, bias_v, positions, allowed):
    score_scale = HEAD_DIM ** (-0.5)
    normed, norm_pull = jax.vjp(layer_norm, values, gain_row)
    normed_low = normed.astype(jnp.bfloat16)
    project = matmul(normed_low, weight_qkv).astype(jnp.bfloat16)
    query_raw = project[:, :D].astype(jnp.float32)
    keys_h = project[:, D : 2 * D].reshape(MICRO, FRAMES, HEADS, HEAD_DIM)
    values_h = project[:, 2 * D :].reshape(MICRO, FRAMES, HEADS, HEAD_DIM)
    query_u = (
        ((query_raw + bias_u) * score_scale).astype(jnp.bfloat16).reshape(MICRO, FRAMES, HEADS, HEAD_DIM)
    )
    query_v = (
        ((query_raw + bias_v) * score_scale).astype(jnp.bfloat16).reshape(MICRO, FRAMES, HEADS, HEAD_DIM)
    )
    scores = attn_scores(query_u, query_v, keys_h, positions, allowed)
    row_peak = jnp.max(scores, axis=-1, keepdims=True)
    exp_scores = jnp.exp(scores - row_peak)
    row_total = jnp.sum(exp_scores, axis=-1, keepdims=True)
    prob_low = (exp_scores / row_total).astype(jnp.bfloat16)
    log_total = row_peak + jnp.log(row_total)
    mixed_heads = jnp.einsum("bhij,bjhd->bihd", prob_low, values_h, preferred_element_type=jnp.float32)
    mixed_heads = mixed_heads.reshape(MICRO * FRAMES, D).astype(jnp.bfloat16)
    kept_state = (norm_pull, normed_low, keys_h, values_h, query_u, query_v, log_total, mixed_heads)
    return (matmul(mixed_heads, weight_out), kept_state)


def attn_backward(grad_res, kept_state, weight_qkv, weight_out, positions, allowed):
    norm_pull, normed_low, keys_h, values_h, query_u, query_v, log_total, mixed_heads = kept_state
    score_scale = HEAD_DIM ** (-0.5)
    grad_branch = grad_res.astype(jnp.bfloat16)
    weight_out_grad = left_product(mixed_heads, grad_branch)
    grad_mixed = (
        right_product(grad_branch, weight_out).astype(jnp.bfloat16).reshape(MICRO, FRAMES, HEADS, HEAD_DIM)
    )
    scores = attn_scores(query_u, query_v, keys_h, positions, allowed)
    probs = jnp.exp(scores - log_total)
    prob_low = probs.astype(jnp.bfloat16)
    grad_vals = jnp.einsum("bhij,bihd->bjhd", prob_low, grad_mixed, preferred_element_type=jnp.float32)
    grad_probs = jnp.einsum(
        "bihd,bjhd->bhij", grad_mixed, values_h, preferred_element_type=jnp.float32
    )
    row_inner = jnp.sum(probs * grad_probs, axis=-1, keepdims=True)
    grad_scores = (probs * (grad_probs - row_inner)).astype(jnp.bfloat16)
    grad_qu = jnp.einsum("bhij,bjhd->bihd", grad_scores, keys_h, preferred_element_type=jnp.float32)
    grad_keys = jnp.einsum("bhij,bihd->bjhd", grad_scores, query_u, preferred_element_type=jnp.float32)
    grad_table = unskew_rows(
        grad_scores.reshape(MICRO * HEADS, FRAMES, FRAMES)
    ).reshape(MICRO, HEADS, FRAMES, 2 * FRAMES - 1)
    grad_qv = jnp.einsum("bhir,rhd->bihd", grad_table, positions, preferred_element_type=jnp.float32)
    grad_pos = jnp.einsum(
        "bhir,bihd->rhd", grad_table, query_v, preferred_element_type=jnp.float32
    ).reshape(2 * FRAMES - 1, D)
    grad_qu = grad_qu.reshape(MICRO * FRAMES, D) * score_scale
    grad_qv = grad_qv.reshape(MICRO * FRAMES, D) * score_scale
    grad_project = jnp.concatenate(
        [grad_qu + grad_qv, grad_keys.reshape(MICRO * FRAMES, D), grad_vals.reshape(MICRO * FRAMES, D)], axis=1
    ).astype(jnp.bfloat16)
    weight_qkv_grad = left_product(normed_low, grad_project)
    grad_normed = right_product(grad_project, weight_qkv)
    grad_values, grad_gain = norm_pull(grad_normed)
    grad_vec = jnp.stack([grad_gain, jnp.sum(grad_qu, axis=0), jnp.sum(grad_qv, axis=0)], axis=0)
    return (grad_values, grad_vec, weight_qkv_grad, weight_out_grad, grad_pos)


def conv_forward(values, gain_row, gain_inner, weight_in, weight_out, kernel_rows, tap_masks):
    normed, norm_pull = jax.vjp(layer_norm, values, gain_row)
    normed_low = normed.astype(jnp.bfloat16)
    gated = matmul(normed_low, weight_in)
    active, inner_pull = jax.vjp(
        partial(conv_inner, tap_masks=tap_masks), gated, gain_inner, kernel_rows
    )
    active_low = active.astype(jnp.bfloat16)
    return (matmul(active_low, weight_out), (norm_pull, normed_low, inner_pull, active_low))


def conv_backward(grad_res, kept_state, weight_in, weight_out):
    norm_pull, normed_low, inner_pull, active_low = kept_state
    grad_branch = grad_res.astype(jnp.bfloat16)
    weight_out_grad = left_product(active_low, grad_branch)
    grad_active = right_product(grad_branch, weight_out)
    grad_gated, grad_inner, grad_taps = inner_pull(grad_active)
    grad_gated_low = grad_gated.astype(jnp.bfloat16)
    weight_in_grad = left_product(normed_low, grad_gated_low)
    grad_normed = right_product(grad_gated_low, weight_in)
    grad_values, grad_gain = norm_pull(grad_normed)
    grad_vec = jnp.concatenate([grad_gain[None], grad_inner[None], grad_taps], axis=0)
    return (grad_values, grad_vec, weight_in_grad, weight_out_grad)


def other_core(d):
    return d + 1 - 2 * (d % 2)


def flip_x(d):
    return d + 2 - 4 * ((d // 2) % 2)


def flip_y(d):
    return d + 4 - 8 * ((d // 4) % 2)


PERM_CORE = [(d, other_core(d)) for d in range(8)]
PERM_X = [(d, flip_x(d)) for d in range(8)]
PERM_Y = [(d, flip_y(d)) for d in range(8)]


def greet(peers):
    barrier = pltpu.get_barrier_semaphore()
    for peer in peers:
        pl.semaphore_signal(barrier, inc=1, device_id=peer, device_id_type=MESH)
    pl.semaphore_wait(barrier, len(peers))


def rows_of(start, count):
    return pl.ds(pl.multiple_of(start, 16), count)


def gather_kernel(n, count, *refs):
    shards = refs[: count + 1]
    fulls = refs[count + 1 : 2 * count + 2]
    send_sem, recv_sem = refs[2 * count + 2 :]
    z = lax.axis_index("fsdp")
    d = lax.axis_index("dp")
    core, place = d % 2, d // 2
    x_peer, y_peer, core_peer = {"dp": flip_x(d)}, {"dp": flip_y(d)}, {"dp": other_core(d)}
    z_peers = [{"fsdp": (z + k) % n} for k in range(1, n)]
    greet(z_peers + [x_peer, y_peer, core_peer])
    used = [0]
    started = []

    def send(src, dst, peer):
        index = used[0]
        used[0] += 1
        copy = pltpu.make_async_remote_copy(
            src_ref=src,
            dst_ref=dst,
            send_sem=send_sem.at[index],
            recv_sem=recv_sem.at[index],
            device_id=peer,
            device_id_type=MESH,
        )
        copy.start()
        started.append(copy)
        return copy

    first = {}
    for t in range(count):
        depth = shards[t].shape[0]
        part = depth // 8
        for k in range(1, n):
            first[t, k] = send(
                shards[t].at[rows_of((core * 4 + place) * part, part), :],
                fulls[t].at[rows_of(z * depth + (core * 4 + place) * part, part), :],
                z_peers[k - 1],
            )
    late = []
    small = shards[count].shape[0]
    for k in range(1, n):
        late.append(send(shards[count], fulls[count].at[rows_of(z * small, small), :], z_peers[k - 1]))
    for t in range(count + 1):
        depth = shards[t].shape[0]
        late.append(send(shards[t], fulls[t].at[rows_of(z * depth, depth), :], core_peer))

    stages = [(t, k) for t in range(count) for k in range(1, n)]
    across, corner = {}, {}

    def piece(t, k, where, half=None):
        depth = shards[t].shape[0]
        part = depth // 8
        start = ((z + n - k) % n) * depth + (core * 4 + where) * part
        if half is None:
            return fulls[t].at[rows_of(start, part), :]
        return fulls[t].at[rows_of(start + half * (part // 2), part // 2), :]

    flip_1 = place + 1 - 2 * (place % 2)
    flip_2 = place + 2 - 4 * (place // 2)
    for i in range(len(stages) + 2):
        if i < len(stages):
            t, k = stages[i]
            first[t, k].wait_recv()
            mine = piece(t, k, place)
            across[i] = (send(mine, mine, x_peer), send(mine, mine, y_peer))
        if 0 <= i - 1 < len(stages):
            t, k = stages[i - 1]
            by_x, by_y = across[i - 1]
            by_y.wait_recv()
            view = piece(t, k, flip_2, 0)
            one = send(view, view, x_peer)
            by_x.wait_recv()
            view = piece(t, k, flip_1, 1)
            corner[i - 1] = (one, send(view, view, y_peer))
        if 0 <= i - 2 < len(stages):
            t, k = stages[i - 2]
            for copy in corner[i - 2]:
                copy.wait_recv()
            depth = shards[t].shape[0]
            half = depth // 2
            view = fulls[t].at[rows_of(((z + n - k) % n) * depth + core * half, half), :]
            late.append(send(view, view, core_peer))
    for copy in late:
        copy.wait_recv()
    for copy in started:
        copy.wait_send()


def gather_all(n, shards, small, collective_id):
    count = len(shards)
    given = list(shards) + [small]
    copies = count * (n - 1) * 6 + (n - 1) + count + 1
    return pl.pallas_call(
        partial(gather_kernel, n, count),
        out_shape=[jax.ShapeDtypeStruct((n * s.shape[0], s.shape[1]), s.dtype) for s in given],
        in_specs=[pl.BlockSpec(memory_space=pltpu.HBM)] * (count + 1),
        out_specs=[pl.BlockSpec(memory_space=pltpu.HBM)] * (count + 1),
        scratch_shapes=[pltpu.SemaphoreType.DMA((copies,)), pltpu.SemaphoreType.DMA((copies,))],
        compiler_params=pltpu.CompilerParams(collective_id=collective_id, has_side_effects=True),
        name="gather_weights",
    )(*given)


def spread_kernel(count, *refs):
    pieces = refs[:count]
    wholes = refs[count : 2 * count]
    send_sem, recv_sem, own_sem = refs[2 * count :]
    d = lax.axis_index("dp")
    core, place = d % 2, d // 2
    x_peer, y_peer, core_peer = {"dp": flip_x(d)}, {"dp": flip_y(d)}, {"dp": other_core(d)}
    greet([x_peer, y_peer, core_peer])
    used = [0]
    started = []

    def send(src, dst, peer):
        index = used[0]
        used[0] += 1
        copy = pltpu.make_async_remote_copy(
            src_ref=src,
            dst_ref=dst,
            send_sem=send_sem.at[index],
            recv_sem=recv_sem.at[index],
            device_id=peer,
            device_id_type=MESH,
        )
        copy.start()
        started.append(copy)
        return copy

    flip_1 = place + 1 - 2 * (place % 2)
    flip_2 = place + 2 - 4 * (place // 2)

    def region(t, owner_core, where, half=None):
        part = pieces[t].shape[0]
        start = (owner_core * 4 + where) * part
        if half is None:
            return wholes[t].at[rows_of(start, part), :]
        return wholes[t].at[rows_of(start + half * (part // 2), part // 2), :]

    across, own, late = [], [], []
    for t in range(count):
        spot = region(t, core, place)
        across.append((send(pieces[t], spot, x_peer), send(pieces[t], spot, y_peer)))
        late.append(send(pieces[t], spot, core_peer))
        keep = pltpu.make_async_copy(pieces[t], spot, own_sem.at[t])
        keep.start()
        own.append(keep)
    corner = []
    for t in range(count):
        by_x, by_y = across[t]
        by_y.wait_recv()
        view = region(t, core, flip_2, 0)
        one = send(view, view, x_peer)
        view = region(t, core, flip_2)
        late.append(send(view, view, core_peer))
        by_x.wait_recv()
        view = region(t, core, flip_1, 1)
        corner.append((one, send(view, view, y_peer)))
        view = region(t, core, flip_1)
        late.append(send(view, view, core_peer))
    for t in range(count):
        for copy in corner[t]:
            copy.wait_recv()
        view = region(t, core, 3 - place)
        late.append(send(view, view, core_peer))
    for copy in own:
        copy.wait()
    for copy in late:
        copy.wait_recv()
    for copy in started:
        copy.wait_send()


def spread_all(pieces, collective_id):
    count = len(pieces)
    return pl.pallas_call(
        partial(spread_kernel, count),
        out_shape=[jax.ShapeDtypeStruct((8 * s.shape[0], s.shape[1]), s.dtype) for s in pieces],
        in_specs=[pl.BlockSpec(memory_space=pltpu.VMEM)] * count,
        out_specs=[pl.BlockSpec(memory_space=pltpu.HBM)] * count,
        scratch_shapes=[
            pltpu.SemaphoreType.DMA((8 * count,)),
            pltpu.SemaphoreType.DMA((8 * count,)),
            pltpu.SemaphoreType.DMA((count,)),
        ],
        compiler_params=pltpu.CompilerParams(collective_id=collective_id, has_side_effects=True),
        name="spread_sums",
    )(*pieces)


def pick(values, index, axis):
    return lax.dynamic_index_in_dim(values, index, axis, keepdims=False)


def reduce_pieces(n, grad, x_first):
    rows, cols = grad.shape
    part = rows // (8 * n)
    z = lax.axis_index("fsdp")
    d = lax.axis_index("dp")
    core, x_bit, y_bit = d % 2, (d // 2) % 2, d // 4
    held = grad.astype(jnp.bfloat16).reshape(n, 2, 2, 2, part, cols)
    steps = [(PERM_X, x_bit, 2), (PERM_Y, y_bit, 1)] if x_first else [(PERM_Y, y_bit, 1), (PERM_X, x_bit, 1)]
    for perm, bit, axis in [(PERM_CORE, core, 1)] + steps:
        got = lax.ppermute(pick(held, 1 - bit, axis), "dp", perm)
        kept = pick(held, bit, axis)
        held = (kept.astype(jnp.float32) + got.astype(jnp.float32)).astype(jnp.bfloat16)
    total = pick(held, z, 0).astype(jnp.float32)
    for k in range(1, n):
        got = lax.ppermute(pick(held, (z + k) % n, 0), "fsdp", [(i, (i + k) % n) for i in range(n)])
        total = total + got.astype(jnp.float32)
    return total.astype(jnp.bfloat16)


def reduce_small(n, grad):
    width = grad.shape[1] // n
    z = lax.axis_index("fsdp")
    for perm in (PERM_CORE, PERM_X, PERM_Y):
        grad = grad + lax.ppermute(grad, "dp", perm)
    total = lax.dynamic_slice_in_dim(grad, z * width, width, 1)
    for k in range(1, n):
        mine = lax.dynamic_slice_in_dim(grad, ((z + k) % n) * width, width, 1)
        total = total + lax.ppermute(mine, "fsdp", [(i, (i + k) % n) for i in range(n)])
    return total

def fallback_reduce(grad):
    part = lax.psum_scatter(grad.astype(jnp.bfloat16), "fsdp", scatter_dimension=0, tiled=True)
    return lax.psum(part, "dp")


def on_device(
    fast,
    n,
    inputs,
    cotangent,
    lengths,
    buckets,
    ffn1_in,
    ffn1_out,
    attn_in,
    attn_out,
    conv_in,
    conv_out,
    ffn2_in,
    ffn2_out,
    norm_gains,
    pos_bias,
    kernel,
):
    shards = [ffn1_in, ffn1_out, attn_in, attn_out, conv_in, conv_out, ffn2_in, ffn2_out]
    width = norm_gains.shape[1]
    vectors = jnp.concatenate(
        [norm_gains, pos_bias, kernel, jnp.zeros((3, width), norm_gains.dtype)], axis=0
    )
    if fast:
        gathered = gather_all(n, shards, vectors, 0)
        weights, vec = gathered[:8], gathered[8]
        vec = vec.reshape(n, 16, width).transpose(1, 0, 2).reshape(16, D)
    else:
        weights = [lax.all_gather(s, "fsdp", axis=0, tiled=True) for s in shards]
        vec = lax.all_gather(vectors, "fsdp", axis=1, tiled=True)
    vec = vec.astype(jnp.float32)
    gains, biases, taps = vec[0:6], vec[6:8], vec[8:13]
    plans = [frame_plan(lengths[m], buckets[m]) for m in range(MICRO)]
    allowed = jnp.stack([p[0] for p in plans], axis=0)
    tap_masks = jnp.concatenate([p[1] for p in plans], axis=1)
    table_low = sinusoid().astype(jnp.bfloat16)

    def reduced(grad, x_first):
        if fast:
            return reduce_pieces(n, grad, x_first)
        return fallback_reduce(grad)

    stream = inputs.astype(jnp.float32)
    branch, kept_one = ffn_forward(stream, gains[0], weights[0], weights[1])
    section_one = stream + 0.5 * branch
    positions = (
        matmul(table_low, weights[2][:, 3 * D :])
        .astype(jnp.bfloat16)
        .reshape(2 * FRAMES - 1, HEADS, HEAD_DIM)
    )
    weight_qkv = weights[2][:, : 3 * D]
    branch, kept_two = attn_forward(
        section_one, gains[1], weight_qkv, weights[3], biases[0], biases[1], positions, allowed
    )
    section_two = section_one + branch
    branch, kept_three = conv_forward(
        section_two, gains[2], gains[3], weights[4], weights[5], taps, tap_masks
    )
    section_three = section_two + branch
    branch, kept_four = ffn_forward(section_three, gains[4], weights[6], weights[7])
    section_four = section_three + 0.5 * branch
    final_out, final_pull = jax.vjp(layer_norm, section_four, gains[5])
    grad_stream, grad_final = final_pull(cotangent.astype(jnp.float32))

    grad_values, grad_vec4, grad_in4, grad_out4 = ffn_backward(
        0.5 * grad_stream, kept_four, weights[6], weights[7]
    )
    sums = [None] * 8
    sums[7] = reduced(grad_out4, False)
    sums[6] = reduced(grad_in4, True)
    grad_stream = grad_stream + grad_values
    grad_values, grad_vec3, grad_in3, grad_out3 = conv_backward(
        grad_stream, kept_three, weights[4], weights[5]
    )
    sums[5] = reduced(grad_out3, False)
    sums[4] = reduced(grad_in3, False)
    grad_stream = grad_stream + grad_values
    grad_values, grad_vec2, grad_in2, grad_out2, grad_pos = attn_backward(
        grad_stream, kept_two, weight_qkv, weights[3], positions, allowed
    )
    weight_pos_grad = left_product(table_low, grad_pos.astype(jnp.bfloat16))
    sums[3] = reduced(grad_out2, False)
    sums[2] = reduced(jnp.concatenate([grad_in2, weight_pos_grad], axis=1), True)
    grad_stream = grad_stream + grad_values
    grad_values, grad_vec1, grad_in1, grad_out1 = ffn_backward(
        0.5 * grad_stream, kept_one, weights[0], weights[1]
    )
    sums[1] = reduced(grad_out1, False)
    sums[0] = reduced(grad_in1, True)
    grad_stream = grad_stream + grad_values

    grad_vectors = jnp.concatenate(
        [
            grad_vec1,
            grad_vec2[0:1],
            grad_vec3[0:2],
            grad_vec4,
            grad_final[None],
            grad_vec2[1:3],
            grad_vec3[2:7],
            jnp.zeros((3, D), jnp.float32),
        ],
        axis=0,
    )
    if fast:
        grad_small = reduce_small(n, grad_vectors)
        sums = spread_all(sums, 1)
    else:
        grad_small = lax.psum(
            lax.psum_scatter(grad_vectors, "fsdp", scatter_dimension=1, tiled=True), "dp"
        )
    grads = [s.astype(jnp.float32) for s in sums]
    return (
        final_out.astype(jnp.bfloat16),
        grad_stream,
        *grads,
        grad_small[0:6],
        grad_small[6:8],
        grad_small[8:13],
    )


def solution(mesh):
    in_specs = (
        P(("dp", "fsdp"), None),
        P(("dp", "fsdp"), None),
        P(("dp", "fsdp"), None),
        P(("dp", "fsdp")),
        P("fsdp", None),
        P("fsdp", None),
        P("fsdp", None),
        P("fsdp", None),
        P("fsdp", None),
        P("fsdp", None),
        P("fsdp", None),
        P("fsdp", None),
        P(None, "fsdp"),
        P(None, "fsdp"),
        P(None, "fsdp"),
    )
    out_specs = (
        P(("dp", "fsdp"), None),
        P(("dp", "fsdp"), None),
        P("fsdp", None),
        P("fsdp", None),
        P("fsdp", None),
        P("fsdp", None),
        P("fsdp", None),
        P("fsdp", None),
        P("fsdp", None),
        P("fsdp", None),
        P(None, "fsdp"),
        P(None, "fsdp"),
        P(None, "fsdp"),
    )
    sizes = dict(mesh.shape)
    n = sizes["fsdp"]
    fast = sizes["dp"] == 8 and n == 4
    return jax.shard_map(
        partial(on_device, fast, n), mesh=mesh, in_specs=in_specs, out_specs=out_specs, check_vma=False
    )
```

```python
from functools import partial
import math

import jax
import jax.numpy as jnp
from jax import lax
from jax.experimental import pallas as pl
from jax.experimental.pallas import tpu as pltpu
from jax.sharding import PartitionSpec as P

MESH = pl.DeviceIdType.MESH

D = 1024
HEADS = 8
HEAD_DIM = 128
KERNEL = 5
BUCKET = 64
MICRO = 2
FRAMES = 192
SLOTS = 3


def matmul(left_side, right_side):
    return jnp.dot(left_side, right_side, preferred_element_type=jnp.float32)


def left_product(left_side, right_side):
    return lax.dot_general(
        left_side, right_side, (((0,), (0,)), ((), ())), preferred_element_type=jnp.float32
    )


def right_product(left_side, right_side):
    return lax.dot_general(
        left_side, right_side, (((1,), (1,)), ((), ())), preferred_element_type=jnp.float32
    )


def layer_norm(values, gain_row):
    centred = values - jnp.mean(values, axis=-1, keepdims=True)
    spread = jnp.mean(centred * centred, axis=-1, keepdims=True)
    return centred * lax.rsqrt(spread + 1e-05) * gain_row


def swish_act(values):
    return values * jax.nn.sigmoid(values)


def neighbour(values, offset):
    if offset > 0:
        filler = jnp.zeros((offset,) + values.shape[1:], values.dtype)
        return jnp.concatenate([values[offset:], filler], axis=0)
    if offset < 0:
        filler = jnp.zeros((-offset,) + values.shape[1:], values.dtype)
        return jnp.concatenate([filler, values[:offset]], axis=0)
    return values


def frame_plan(utter_len, bucket_id):
    position = jnp.arange(FRAMES, dtype=jnp.int32)
    bucket_len = BUCKET * (bucket_id + 1)
    segment = position // bucket_len
    offset_in = position - segment * bucket_len
    slot_index = jnp.arange(SLOTS, dtype=jnp.int32)
    slot_limit = jnp.sum(
        jnp.where(segment[:, None] == slot_index[None, :], utter_len[None, :], 0), axis=1
    )
    is_valid = offset_in < slot_limit
    allowed = (segment[:, None] == segment[None, :]) & is_valid[None, :] | (
        position[:, None] == position[None, :]
    )
    tap_list = []
    for tap_index in range(KERNEL):
        shift_by = tap_index - KERNEL // 2
        same_slot = (neighbour(segment + 1, shift_by) == segment + 1) & neighbour(
            is_valid, shift_by
        )
        tap_list.append(same_slot.astype(jnp.float32))
    return (allowed, jnp.stack(tap_list, axis=0))


def sinusoid(sign):
    column = jnp.arange(D, dtype=jnp.int32)
    rates = jnp.exp((column // 2).astype(jnp.float32) * (-2.0 * math.log(10000.0) / D))
    phase = (column % 2).astype(jnp.float32) * (0.5 * math.pi)
    coarse = sign * (16 * jnp.arange(2 * FRAMES // 16, dtype=jnp.int32) - (FRAMES - 1)).astype(jnp.float32)
    fine = sign * jnp.arange(16, dtype=jnp.int32).astype(jnp.float32)
    angle = coarse[:, None] * rates[None, :]
    rest = fine[:, None] * rates[None, :] + phase[None, :]
    sin_a, cos_a = lax.optimization_barrier((jnp.sin(angle), jnp.cos(angle)))
    sin_b, cos_b = lax.optimization_barrier((jnp.sin(rest), jnp.cos(rest)))
    table = sin_a[:, None] * cos_b[None] + cos_a[:, None] * sin_b[None]
    return table.reshape(2 * FRAMES, D)


def depthwise(values, kernel_rows, tap_masks):
    running = jnp.zeros_like(values)
    for tap_index in range(KERNEL):
        moved = neighbour(values, tap_index - KERNEL // 2)
        running = running + moved * tap_masks[tap_index][:, None] * kernel_rows[tap_index][None, :]
    return running


def conv_inner(gated, gain_inner, kernel_rows, tap_masks):
    gated_out = gated[:, :D] * jax.nn.sigmoid(gated[:, D:])
    return swish_act(layer_norm(depthwise(gated_out, kernel_rows, tap_masks), gain_inner))


def ffn_forward(values, gain_row, weight_in, weight_out):
    normed, norm_pull = jax.vjp(layer_norm, values, gain_row)
    normed_low = normed.astype(jnp.bfloat16)
    hidden = matmul(normed_low, weight_in)
    active = swish_act(hidden).astype(jnp.bfloat16)
    return (matmul(active, weight_out), (norm_pull, normed_low, hidden, active))


def ffn_backward(grad_branch, kept_state, weight_in, weight_out):
    norm_pull, normed_low, hidden, active = kept_state
    grad_out = grad_branch.astype(jnp.bfloat16)
    grad_active = right_product(grad_out, weight_out)
    swish_value, swish_pull = jax.vjp(swish_act, hidden)
    grad_hidden = swish_pull(grad_active)[0].astype(jnp.bfloat16)
    grad_normed = right_product(grad_hidden, weight_in)
    grad_values, grad_gain = norm_pull(grad_normed)
    return (grad_values, grad_gain[None], [(normed_low, grad_hidden)], [(active, grad_out)])


TABLE = 2 * FRAMES
SCALE = HEAD_DIM ** (-0.5)


def nn(left_side, right_side):
    return lax.dot_general(
        left_side, right_side, (((1,), (0,)), ((), ())), preferred_element_type=jnp.float32
    )


def attend_kernel(q_ref, k_ref, v_ref, bias_ref, pos_ref, allow_ref, mixed_ref, prob_ref):
    query = q_ref[...].astype(jnp.float32)
    query_u = ((query + bias_ref[0:1, :]) * SCALE).astype(jnp.bfloat16)
    query_v = ((query + bias_ref[1:2, :]) * SCALE).astype(jnp.bfloat16)
    table = right_product(query_v, pos_ref[...])
    for m in range(MICRO):
        rows = slice(m * FRAMES, (m + 1) * FRAMES)
        content = right_product(query_u[rows], k_ref[rows, :])
        moved = pltpu.roll(table[rows], TABLE - FRAMES + 1, 1, stride=1, stride_axis=0)
        scores = jnp.where(allow_ref[m] > 0, content + moved[:, :FRAMES], -1e30)
        weight = jnp.exp(scores - jnp.max(scores, axis=-1, keepdims=True))
        prob = (weight / jnp.sum(weight, axis=-1, keepdims=True)).astype(jnp.bfloat16)
        prob_ref[m, 0] = prob
        mixed_ref[rows, :] = nn(prob, v_ref[rows, :]).astype(jnp.bfloat16)


def attend_back_kernel(
    q_ref, k_ref, v_ref, bias_ref, pos_ref, prob_ref, grad_ref, dq_ref, dk_ref, dv_ref, dpos_ref, dbias_ref
):
    query = q_ref[...].astype(jnp.float32)
    query_u = ((query + bias_ref[0:1, :]) * SCALE).astype(jnp.bfloat16)
    query_v = ((query + bias_ref[1:2, :]) * SCALE).astype(jnp.bfloat16)
    across = lax.broadcasted_iota(jnp.int32, (FRAMES, FRAMES), 0)
    down = lax.broadcasted_iota(jnp.int32, (FRAMES, FRAMES), 1)
    swap = jnp.where(across + down == FRAMES - 1, 1.0, 0.0).astype(jnp.bfloat16)
    tables, grads_u = [], []
    for m in range(MICRO):
        rows = slice(m * FRAMES, (m + 1) * FRAMES)
        prob = prob_ref[m, 0]
        grad = grad_ref[rows, :]
        dv_ref[rows, :] = left_product(prob, grad).astype(jnp.bfloat16)
        grad_prob = right_product(grad, v_ref[rows, :])
        wide = prob.astype(jnp.float32)
        inner = jnp.sum(wide * grad_prob, axis=-1, keepdims=True)
        grad_score = wide * (grad_prob - inner)
        low = grad_score.astype(jnp.bfloat16)
        grads_u.append(nn(low, k_ref[rows, :]))
        dk_ref[rows, :] = left_product(low, query_u[rows]).astype(jnp.bfloat16)
        turned = nn(low, swap)
        padded = jnp.concatenate([turned, jnp.zeros_like(turned)], axis=1)
        tables.append(pltpu.roll(padded, 0, 1, stride=1, stride_axis=0))
    table = jnp.concatenate(tables, axis=0).astype(jnp.bfloat16)
    grad_u = jnp.concatenate(grads_u, axis=0) * SCALE
    grad_v = nn(table, pos_ref[...]) * SCALE
    dpos_ref[...] = left_product(table, query_v).astype(jnp.bfloat16)
    dq_ref[...] = (grad_u + grad_v).astype(jnp.bfloat16)
    dbias_ref[0:1, :] = jnp.sum(grad_u, axis=0, keepdims=True)
    dbias_ref[1:2, :] = jnp.sum(grad_v, axis=0, keepdims=True)


def head_spec(rows, offset=0):
    return pl.BlockSpec((rows, HEAD_DIM), lambda h: (0, offset + h))


PROB_SPEC = pl.BlockSpec((MICRO, 1, FRAMES, FRAMES), lambda h: (0, h, 0, 0))


def attend(project, bias, positions, allowed):
    rows = project.shape[0]
    return pl.pallas_call(
        attend_kernel,
        grid=(HEADS,),
        out_shape=[
            jax.ShapeDtypeStruct((rows, D), jnp.bfloat16),
            jax.ShapeDtypeStruct((MICRO, HEADS, FRAMES, FRAMES), jnp.bfloat16),
        ],
        in_specs=[
            head_spec(rows),
            head_spec(rows, HEADS),
            head_spec(rows, 2 * HEADS),
            head_spec(2),
            head_spec(TABLE),
            pl.BlockSpec((MICRO, FRAMES, FRAMES), lambda h: (0, 0, 0)),
        ],
        out_specs=[head_spec(rows), PROB_SPEC],
        name="attend",
    )(project, project, project, bias, positions, allowed)


def attend_back(project, bias, positions, prob, grad_mixed):
    rows = project.shape[0]
    wide = jax.ShapeDtypeStruct((rows, D), jnp.bfloat16)
    return pl.pallas_call(
        attend_back_kernel,
        grid=(HEADS,),
        out_shape=[
            wide,
            wide,
            wide,
            jax.ShapeDtypeStruct((TABLE, D), jnp.bfloat16),
            jax.ShapeDtypeStruct((2, D), jnp.float32),
        ],
        in_specs=[
            head_spec(rows),
            head_spec(rows, HEADS),
            head_spec(rows, 2 * HEADS),
            head_spec(2),
            head_spec(TABLE),
            PROB_SPEC,
            head_spec(rows),
        ],
        out_specs=[head_spec(rows), head_spec(rows), head_spec(rows), head_spec(TABLE), head_spec(2)],
        name="attend_back",
    )(project, project, project, bias, positions, prob, grad_mixed)


def attn_forward(values, gain_row, weight_qkv, weight_out, bias, positions, allowed):
    normed, norm_pull = jax.vjp(layer_norm, values, gain_row)
    normed_low = normed.astype(jnp.bfloat16)
    project = matmul(normed_low, weight_qkv).astype(jnp.bfloat16)
    mixed_heads, prob = attend(project, bias, positions, allowed)
    kept_state = (norm_pull, normed_low, project, prob, mixed_heads)
    return (matmul(mixed_heads, weight_out), kept_state)


def attn_backward(grad_res, kept_state, weight_qkv, weight_out, bias, positions):
    norm_pull, normed_low, project, prob, mixed_heads = kept_state
    grad_branch = grad_res.astype(jnp.bfloat16)
    grad_mixed = right_product(grad_branch, weight_out).astype(jnp.bfloat16)
    grad_q, grad_k, grad_v, grad_pos, grad_bias = attend_back(
        project, bias, positions, prob, grad_mixed
    )
    grad_project = jnp.concatenate([grad_q, grad_k, grad_v], axis=1)
    grad_normed = right_product(grad_project, weight_qkv)
    grad_values, grad_gain = norm_pull(grad_normed)
    grad_vec = jnp.concatenate([grad_gain[None], grad_bias], axis=0)
    return (grad_values, grad_vec, [(normed_low, grad_project)], [(mixed_heads, grad_branch)], grad_pos)


def conv_forward(values, gain_row, gain_inner, weight_in, weight_out, kernel_rows, tap_masks):
    normed, norm_pull = jax.vjp(layer_norm, values, gain_row)
    normed_low = normed.astype(jnp.bfloat16)
    gated = matmul(normed_low, weight_in)
    active, inner_pull = jax.vjp(
        partial(conv_inner, tap_masks=tap_masks), gated, gain_inner, kernel_rows
    )
    active_low = active.astype(jnp.bfloat16)
    return (matmul(active_low, weight_out), (norm_pull, normed_low, inner_pull, active_low))


def conv_backward(grad_res, kept_state, weight_in, weight_out):
    norm_pull, normed_low, inner_pull, active_low = kept_state
    grad_branch = grad_res.astype(jnp.bfloat16)
    grad_active = right_product(grad_branch, weight_out)
    grad_gated, grad_inner, grad_taps = inner_pull(grad_active)
    grad_gated_low = grad_gated.astype(jnp.bfloat16)
    grad_normed = right_product(grad_gated_low, weight_in)
    grad_values, grad_gain = norm_pull(grad_normed)
    grad_vec = jnp.concatenate([grad_gain[None], grad_inner[None], grad_taps], axis=0)
    return (grad_values, grad_vec, [(normed_low, grad_gated_low)], [(active_low, grad_branch)])


def other_core(d):
    return d + 1 - 2 * (d % 2)


def flip_x(d):
    return d + 2 - 4 * ((d // 2) % 2)


def flip_y(d):
    return d + 4 - 8 * ((d // 4) % 2)


def greet(peers):
    barrier = pltpu.get_barrier_semaphore()
    for peer in peers:
        pl.semaphore_signal(barrier, inc=1, device_id=peer, device_id_type=MESH)
    pl.semaphore_wait(barrier, len(peers))


def rows_of(start, count):
    return pl.ds(pl.multiple_of(start, 16), count)


def gather_kernel(n, count, *refs):
    shards = refs[: count + 1]
    fulls = refs[count + 1 : 2 * count + 2]
    send_sem, recv_sem = refs[2 * count + 2 :]
    z = lax.axis_index("fsdp")
    d = lax.axis_index("dp")
    core, place = d % 2, d // 2
    x_peer, y_peer, core_peer = {"dp": flip_x(d)}, {"dp": flip_y(d)}, {"dp": other_core(d)}
    z_peers = [{"fsdp": (z + k) % n} for k in range(1, n)]
    greet(z_peers + [x_peer, y_peer, core_peer])
    used = [0]
    started = []

    def send(src, dst, peer):
        index = used[0]
        used[0] += 1
        copy = pltpu.make_async_remote_copy(
            src_ref=src,
            dst_ref=dst,
            send_sem=send_sem.at[index],
            recv_sem=recv_sem.at[index],
            device_id=peer,
            device_id_type=MESH,
        )
        copy.start()
        started.append(copy)
        return copy

    first = {}
    for t in range(count):
        depth = shards[t].shape[0]
        part = depth // 8
        for k in range(1, n):
            first[t, k] = send(
                shards[t].at[rows_of((core * 4 + place) * part, part), :],
                fulls[t].at[rows_of(z * depth + (core * 4 + place) * part, part), :],
                z_peers[k - 1],
            )
    late = []
    small = shards[count].shape[0]
    for k in range(1, n):
        late.append(send(shards[count], fulls[count].at[rows_of(z * small, small), :], z_peers[k - 1]))
    for t in range(count + 1):
        depth = shards[t].shape[0]
        late.append(send(shards[t], fulls[t].at[rows_of(z * depth, depth), :], core_peer))

    stages = [(t, k) for t in range(count) for k in range(1, n)]
    across, corner = {}, {}

    def piece(t, k, where, half=None):
        depth = shards[t].shape[0]
        part = depth // 8
        start = ((z + n - k) % n) * depth + (core * 4 + where) * part
        if half is None:
            return fulls[t].at[rows_of(start, part), :]
        return fulls[t].at[rows_of(start + half * (part // 2), part // 2), :]

    flip_1 = place + 1 - 2 * (place % 2)
    flip_2 = place + 2 - 4 * (place // 2)
    for i in range(len(stages) + 2):
        if i < len(stages):
            t, k = stages[i]
            first[t, k].wait_recv()
            mine = piece(t, k, place)
            across[i] = (send(mine, mine, x_peer), send(mine, mine, y_peer))
        if 0 <= i - 1 < len(stages):
            t, k = stages[i - 1]
            by_x, by_y = across[i - 1]
            by_y.wait_recv()
            view = piece(t, k, flip_2, 0)
            one = send(view, view, x_peer)
            by_x.wait_recv()
            view = piece(t, k, flip_1, 1)
            corner[i - 1] = (one, send(view, view, y_peer))
        if 0 <= i - 2 < len(stages):
            t, k = stages[i - 2]
            for copy in corner[i - 2]:
                copy.wait_recv()
            depth = shards[t].shape[0]
            half = depth // 2
            view = fulls[t].at[rows_of(((z + n - k) % n) * depth + core * half, half), :]
            late.append(send(view, view, core_peer))
    for copy in late:
        copy.wait_recv()
    for copy in started:
        copy.wait_send()


def gather_all(n, shards, small, collective_id):
    count = len(shards)
    given = list(shards) + [small]
    copies = count * (n - 1) * 6 + (n - 1) + count + 1
    return pl.pallas_call(
        partial(gather_kernel, n, count),
        out_shape=[jax.ShapeDtypeStruct((n * s.shape[0], s.shape[1]), s.dtype) for s in given],
        in_specs=[pl.BlockSpec(memory_space=pltpu.HBM)] * (count + 1),
        out_specs=[pl.BlockSpec(memory_space=pltpu.HBM)] * (count + 1),
        scratch_shapes=[pltpu.SemaphoreType.DMA((copies,)), pltpu.SemaphoreType.DMA((copies,))],
        compiler_params=pltpu.CompilerParams(collective_id=collective_id, has_side_effects=True),
        name="gather_weights",
    )(*given)


def spread_kernel(count, *refs):
    pieces = refs[:count]
    wholes = refs[count : 2 * count]
    send_sem, recv_sem, own_sem = refs[2 * count :]
    d = lax.axis_index("dp")
    core, place = d % 2, d // 2
    x_peer, y_peer, core_peer = {"dp": flip_x(d)}, {"dp": flip_y(d)}, {"dp": other_core(d)}
    greet([x_peer, y_peer, core_peer])
    used = [0]
    started = []

    def send(src, dst, peer):
        index = used[0]
        used[0] += 1
        copy = pltpu.make_async_remote_copy(
            src_ref=src,
            dst_ref=dst,
            send_sem=send_sem.at[index],
            recv_sem=recv_sem.at[index],
            device_id=peer,
            device_id_type=MESH,
        )
        copy.start()
        started.append(copy)
        return copy

    flip_1 = place + 1 - 2 * (place % 2)
    flip_2 = place + 2 - 4 * (place // 2)

    def region(t, owner_core, where, half=None):
        part = pieces[t].shape[0]
        start = (owner_core * 4 + where) * part
        if half is None:
            return wholes[t].at[rows_of(start, part), :]
        return wholes[t].at[rows_of(start + half * (part // 2), part // 2), :]

    across, own, late = [], [], []
    for t in range(count):
        spot = region(t, core, place)
        across.append((send(pieces[t], spot, x_peer), send(pieces[t], spot, y_peer)))
        late.append(send(pieces[t], spot, core_peer))
        keep = pltpu.make_async_copy(pieces[t], spot, own_sem.at[t])
        keep.start()
        own.append(keep)
    corner = []
    for t in range(count):
        by_x, by_y = across[t]
        by_y.wait_recv()
        view = region(t, core, flip_2, 0)
        one = send(view, view, x_peer)
        view = region(t, core, flip_2)
        late.append(send(view, view, core_peer))
        by_x.wait_recv()
        view = region(t, core, flip_1, 1)
        corner.append((one, send(view, view, y_peer)))
        view = region(t, core, flip_1)
        late.append(send(view, view, core_peer))
    for t in range(count):
        for copy in corner[t]:
            copy.wait_recv()
        view = region(t, core, 3 - place)
        late.append(send(view, view, core_peer))
    for copy in own:
        copy.wait()
    for copy in late:
        copy.wait_recv()
    for copy in started:
        copy.wait_send()


def spread_all(pieces, collective_id):
    count = len(pieces)
    return pl.pallas_call(
        partial(spread_kernel, count),
        out_shape=[jax.ShapeDtypeStruct((8 * s.shape[0], s.shape[1]), s.dtype) for s in pieces],
        in_specs=[pl.BlockSpec(memory_space=pltpu.VMEM)] * count,
        out_specs=[pl.BlockSpec(memory_space=pltpu.HBM)] * count,
        scratch_shapes=[
            pltpu.SemaphoreType.DMA((8 * count,)),
            pltpu.SemaphoreType.DMA((8 * count,)),
            pltpu.SemaphoreType.DMA((count,)),
        ],
        compiler_params=pltpu.CompilerParams(collective_id=collective_id, has_side_effects=True),
        name="spread_sums",
    )(*pieces)


def add_rows(dst, dst_row, src, src_row, count):
    @pl.loop(0, count // 16)
    def _(step):
        at = pl.ds(pl.multiple_of(dst_row + step * 16, 16), 16)
        take = pl.ds(pl.multiple_of(src_row + step * 16, 16), 16)
        total = dst[at, :].astype(jnp.float32) + src[take, :].astype(jnp.float32)
        dst[at, :] = total.astype(jnp.bfloat16)


def sums_kernel(n, plan, small, *refs):
    count = len(plan)
    inputs = sum(2 * len(widths) for _, widths in plan)
    operands = list(refs[:inputs])
    refs = refs[inputs:]
    if small:
        small_ref, refs = refs[0], refs[1:]
    outs, refs = refs[:count], refs[count:]
    if small:
        small_out, refs = refs[0], refs[1:]
    held, refs = refs[:count], refs[count:]
    from_core, refs = refs[:count], refs[count:]
    from_first, refs = refs[:count], refs[count:]
    from_second, refs = refs[:count], refs[count:]
    from_z, refs = refs[:count], refs[count:]
    if small:
        (small_held, small_got, small_z), refs = refs[:3], refs[3:]
    send_sem, recv_sem = refs
    pairs = []
    for _, widths in plan:
        pairs.append([(operands.pop(0), operands.pop(0)) for _ in widths])
    z = lax.axis_index("fsdp")
    d = lax.axis_index("dp")
    core, place = d % 2, d // 2
    x_bit, y_bit = place % 2, place // 2
    peers = [{"dp": flip_x(d)}, {"dp": flip_y(d)}]
    core_peer = {"dp": other_core(d)}
    z_peers = [{"fsdp": (z + k) % n} for k in range(1, n)]
    greet(z_peers + peers + [core_peer])
    used = [0]
    started = []

    def send(src, dst, peer, keep=True):
        index = used[0]
        used[0] += 1
        copy = pltpu.make_async_remote_copy(
            src_ref=src,
            dst_ref=dst,
            send_sem=send_sem.at[index],
            recv_sem=recv_sem.at[index],
            device_id=peer,
            device_id_type=MESH,
        )
        copy.start()
        if keep:
            started.append(copy)
        return copy

    units = [(t, k) for t in range(count) for k in [*range(1, n), 0]]
    part = [rows // (8 * n) for rows, _ in plan]
    arrive, first, second, third = {}, {}, {}, {}

    def make(t, k, spare):
        half = 4 * part[t]
        tile = 128 * 1024 // half
        column = ((z + k) % n) * 2 * half
        offset = 0
        for (left, right), width in zip(pairs[t], plan[t][1]):
            tiles = width // tile

            @pl.loop(0, 2 * tiles)
            def _(step):
                own, index = step // tiles, step % tiles
                side = own * core + (1 - own) * (1 - core)
                source = pl.ds(pl.multiple_of(column + side * half, 128), half)
                row = own * (k * half) + (1 - own) * ((n + spare) * half)
                across = pl.ds(pl.multiple_of(index * tile, 128), tile)
                target = pl.ds(pl.multiple_of(offset + index * tile, 128), tile)
                block = left_product(left[:, source], right[:, across])
                held[t][rows_of(row, half), target] = block.astype(jnp.bfloat16)

            offset += width

    for i in range(len(units) + 6):
        if i < len(units):
            t, k = units[i]
            half, spare = 4 * part[t], i % 2
            if i >= 2 and units[i - 2][0] == t:
                arrive[i - 2].wait_send()
            make(t, k, spare)
            arrive[i] = send(
                held[t].at[pl.ds((n + spare) * half, half), :],
                from_core[t].at[pl.ds(k * half, half), :],
                core_peer,
                keep=i + 2 >= len(units) or units[i + 2][0] != t,
            )
        if small and i < 3:
            if i == 0:
                small_held[...] = small_ref[...]
            else:
                small_copy.wait()
                small_held[...] += small_got[i - 1]
            small_copy = send(small_held, small_got.at[i], [core_peer, *peers][i], keep=False)
        if small and i == 3:
            small_copy.wait()
            small_held[...] += small_got[2]
            width = small_out.shape[1]
            small_z_copies = [
                send(
                    small_held.at[:, pl.ds(pl.multiple_of(((z + k) % n) * width, 128), width)],
                    small_z.at[k - 1],
                    z_peers[k - 1],
                )
                for k in range(1, n)
            ]
        j = i - 1
        if 0 <= j < len(units):
            t, k = units[j]
            p, base = part[t], k * 4 * part[t]
            arrive[j].wait_recv()
            add_rows(held[t], base, from_core[t], base, 4 * p)
            if j % 2 == 0:
                first[j] = [
                    send(
                        held[t].at[rows_of(base + (2 * y + 1 - x_bit) * p, p), :],
                        from_first[t].at[pl.ds((2 * k + y) * p, p), :],
                        peers[0],
                    )
                    for y in range(2)
                ]
            else:
                first[j] = [
                    send(
                        held[t].at[rows_of(base + 2 * (1 - y_bit) * p, 2 * p), :],
                        from_first[t].at[pl.ds(2 * k * p, 2 * p), :],
                        peers[1],
                    )
                ]
        j = i - 3
        if 0 <= j < len(units):
            t, k = units[j]
            p, base = part[t], k * 4 * part[t]
            for copy in first[j]:
                copy.wait_recv()
            if j % 2 == 0:
                for y in range(2):
                    add_rows(held[t], base + (2 * y + x_bit) * p, from_first[t], (2 * k + y) * p, p)
                gone, peer = base + (2 * (1 - y_bit) + x_bit) * p, peers[1]
            else:
                add_rows(held[t], base + 2 * y_bit * p, from_first[t], 2 * k * p, 2 * p)
                gone, peer = base + (2 * y_bit + 1 - x_bit) * p, peers[0]
            second[j] = send(held[t].at[rows_of(gone, p), :], from_second[t].at[pl.ds(k * p, p), :], peer)
        j = i - 5
        if 0 <= j < len(units):
            t, k = units[j]
            p, base = part[t], k * 4 * part[t]
            second[j].wait_recv()
            add_rows(held[t], base + place * p, from_second[t], k * p, p)
            if k > 0:
                third[t, k] = send(
                    held[t].at[rows_of(base + place * p, p), :],
                    from_z[t].at[pl.ds((k - 1) * p, p), :],
                    z_peers[k - 1],
                )
    for t in range(count):
        p = part[t]
        for k in range(1, n):
            third[t, k].wait_recv()

        @pl.loop(0, p // 16)
        def _(step):
            total = held[t][pl.ds(pl.multiple_of(place * p + step * 16, 16), 16), :].astype(jnp.float32)
            for k in range(1, n):
                at = pl.ds(pl.multiple_of((k - 1) * p + step * 16, 16), 16)
                total = total + from_z[t][at, :].astype(jnp.float32)
            outs[t][pl.ds(pl.multiple_of(step * 16, 16), 16), :] = total.astype(jnp.bfloat16)

    if small:
        for copy in small_z_copies:
            copy.wait_recv()
        total = small_held[:, pl.ds(pl.multiple_of(z * width, 128), width)]
        for k in range(1, n):
            total = total + small_z[k - 1]
        small_out[...] = total
    for copy in started:
        copy.wait_send()


def sum_products(n, tensors, small, collective_id):
    plan = [
        (pairs[0][0].shape[1], tuple(right.shape[1] for _, right in pairs)) for pairs in tensors
    ]
    count = len(plan)
    operands = [side for pairs in tensors for pair in pairs for side in pair]
    shapes = [(rows, sum(widths)) for rows, widths in plan]
    out_shape = [jax.ShapeDtypeStruct((r // (8 * n), c), jnp.bfloat16) for r, c in shapes]

    def room(over, under):
        return [pltpu.VMEM((r * over // under, c), jnp.bfloat16) for r, c in shapes]

    scratch = [
        *room(n + 2, 2 * n),
        *room(1, 2),
        *room(1, 4),
        *room(1, 8),
        *room(n - 1, 8 * n),
    ]
    copies = count * (5 * n - 1)
    if small is not None:
        operands.append(small)
        depth, width = small.shape
        out_shape.append(jax.ShapeDtypeStruct((depth, width // n), jnp.float32))
        scratch += [
            pltpu.VMEM((depth, width), jnp.float32),
            pltpu.VMEM((3, depth, width), jnp.float32),
            pltpu.VMEM((n - 1, depth, width // n), jnp.float32),
        ]
        copies += 3 + n - 1
    whole = pl.BlockSpec(memory_space=pltpu.VMEM)
    return pl.pallas_call(
        partial(sums_kernel, n, plan, small is not None),
        out_shape=out_shape,
        in_specs=[whole] * len(operands),
        out_specs=[whole] * len(out_shape),
        scratch_shapes=[
            *scratch,
            pltpu.SemaphoreType.DMA((copies,)),
            pltpu.SemaphoreType.DMA((copies,)),
        ],
        compiler_params=pltpu.CompilerParams(
            collective_id=collective_id, has_side_effects=True, vmem_limit_bytes=63 * 1024 * 1024
        ),
        name="sum_products",
    )(*operands)


EARLY = (6, 7, 4, 5, 3)
LATE = (2, 0, 1)


def fallback_reduce(pairs):
    grad = jnp.concatenate([left_product(left, right) for left, right in pairs], axis=1)
    part = lax.psum_scatter(grad.astype(jnp.bfloat16), "fsdp", scatter_dimension=0, tiled=True)
    return lax.psum(part, "dp")


def on_device(
    fast,
    n,
    inputs,
    cotangent,
    lengths,
    buckets,
    ffn1_in,
    ffn1_out,
    attn_in,
    attn_out,
    conv_in,
    conv_out,
    ffn2_in,
    ffn2_out,
    norm_gains,
    pos_bias,
    kernel,
):
    shards = [ffn1_in, ffn1_out, attn_in, attn_out, conv_in, conv_out, ffn2_in, ffn2_out]
    width = norm_gains.shape[1]
    vectors = jnp.concatenate(
        [norm_gains, pos_bias, kernel, jnp.zeros((3, width), norm_gains.dtype)], axis=0
    )
    if fast:
        gathered = gather_all(n, shards, vectors, 0)
        weights, vec = gathered[:8], gathered[8]
        vec = vec.reshape(n, 16, width).transpose(1, 0, 2).reshape(16, D)
    else:
        weights = [lax.all_gather(s, "fsdp", axis=0, tiled=True) for s in shards]
        vec = lax.all_gather(vectors, "fsdp", axis=1, tiled=True)
    vec = vec.astype(jnp.float32)
    gains, biases, taps = vec[0:6], vec[6:8], vec[8:13]
    plans = [frame_plan(lengths[m], buckets[m]) for m in range(MICRO)]
    allowed = jnp.stack([p[0] for p in plans], axis=0).astype(jnp.float32)
    tap_masks = jnp.concatenate([p[1] for p in plans], axis=1)
    table_low = sinusoid(1).astype(jnp.bfloat16)
    mirror_low = sinusoid(-1).astype(jnp.bfloat16)

    stream = inputs.astype(jnp.float32)
    branch, kept_one = ffn_forward(stream, gains[0], weights[0], weights[1])
    section_one = stream + 0.5 * branch
    positions = matmul(table_low, weights[2][:, 3 * D :]).astype(jnp.bfloat16)
    mirrored = matmul(mirror_low, weights[2][:, 3 * D :]).astype(jnp.bfloat16)
    weight_qkv = weights[2][:, : 3 * D]
    branch, kept_two = attn_forward(
        section_one, gains[1], weight_qkv, weights[3], biases, positions, allowed
    )
    section_two = section_one + branch
    branch, kept_three = conv_forward(
        section_two, gains[2], gains[3], weights[4], weights[5], taps, tap_masks
    )
    section_three = section_two + branch
    branch, kept_four = ffn_forward(section_three, gains[4], weights[6], weights[7])
    section_four = section_three + 0.5 * branch
    final_out, final_pull = jax.vjp(layer_norm, section_four, gains[5])
    grad_stream, grad_final = final_pull(cotangent.astype(jnp.float32))

    grad_values, grad_vec4, grad_in4, grad_out4 = ffn_backward(
        0.5 * grad_stream, kept_four, weights[6], weights[7]
    )
    sums = [None] * 8
    grad_stream = grad_stream + grad_values
    grad_values, grad_vec3, grad_in3, grad_out3 = conv_backward(
        grad_stream, kept_three, weights[4], weights[5]
    )
    grad_stream = grad_stream + grad_values
    grad_values, grad_vec2, grad_in2, grad_out2, grad_pos = attn_backward(
        grad_stream, kept_two, weight_qkv, weights[3], biases, mirrored
    )
    grad_stream = grad_stream + grad_values
    grad_values, grad_vec1, grad_in1, grad_out1 = ffn_backward(
        0.5 * grad_stream, kept_one, weights[0], weights[1]
    )
    grad_in2 = grad_in2 + [(mirror_low, grad_pos)]
    grad_stream = grad_stream + grad_values

    grad_vectors = jnp.concatenate(
        [
            grad_vec1,
            grad_vec2[0:1],
            grad_vec3[0:2],
            grad_vec4,
            grad_final[None],
            grad_vec2[1:3],
            grad_vec3[2:7],
            jnp.zeros((3, D), jnp.float32),
        ],
        axis=0,
    )
    tensors = [grad_in1, grad_out1, grad_in2, grad_out2, grad_in3, grad_out3, grad_in4, grad_out4]
    if fast:
        early = sum_products(n, [tensors[i] for i in EARLY], None, 2)
        *late, grad_small = sum_products(n, [tensors[i] for i in LATE], grad_vectors, 3)
        for index, total in zip(EARLY + LATE, list(early) + late):
            sums[index] = total
        sums = spread_all(sums, 1)
    else:
        sums = [fallback_reduce(pairs) for pairs in tensors]
        grad_small = lax.psum(
            lax.psum_scatter(grad_vectors, "fsdp", scatter_dimension=1, tiled=True), "dp"
        )
    grads = [s.astype(jnp.float32) for s in sums]
    return (
        final_out.astype(jnp.bfloat16),
        grad_stream,
        *grads,
        grad_small[0:6],
        grad_small[6:8],
        grad_small[8:13],
    )


def solution(mesh):
    in_specs = (
        P(("dp", "fsdp"), None),
        P(("dp", "fsdp"), None),
        P(("dp", "fsdp"), None),
        P(("dp", "fsdp")),
        P("fsdp", None),
        P("fsdp", None),
        P("fsdp", None),
        P("fsdp", None),
        P("fsdp", None),
        P("fsdp", None),
        P("fsdp", None),
        P("fsdp", None),
        P(None, "fsdp"),
        P(None, "fsdp"),
        P(None, "fsdp"),
    )
    out_specs = (
        P(("dp", "fsdp"), None),
        P(("dp", "fsdp"), None),
        P("fsdp", None),
        P("fsdp", None),
        P("fsdp", None),
        P("fsdp", None),
        P("fsdp", None),
        P("fsdp", None),
        P("fsdp", None),
        P("fsdp", None),
        P(None, "fsdp"),
        P(None, "fsdp"),
        P(None, "fsdp"),
    )
    sizes = dict(mesh.shape)
    n = sizes["fsdp"]
    fast = sizes["dp"] == 8 and n == 4
    return jax.shard_map(
        partial(on_device, fast, n), mesh=mesh, in_specs=in_specs, out_specs=out_specs, check_vma=False
    )
```

```python
from functools import partial
import math

import jax
import jax.numpy as jnp
from jax import lax
from jax.experimental import pallas as pl
from jax.experimental.pallas import tpu as pltpu
from jax.sharding import PartitionSpec as P

MESH = pl.DeviceIdType.MESH

D = 1024
HEADS = 8
HEAD_DIM = 128
KERNEL = 5
BUCKET = 64
MICRO = 2
FRAMES = 192
SLOTS = 3


def matmul(left_side, right_side):
    return jnp.dot(left_side, right_side, preferred_element_type=jnp.float32)


def left_product(left_side, right_side):
    return lax.dot_general(
        left_side, right_side, (((0,), (0,)), ((), ())), preferred_element_type=jnp.float32
    )


def right_product(left_side, right_side):
    return lax.dot_general(
        left_side, right_side, (((1,), (1,)), ((), ())), preferred_element_type=jnp.float32
    )


def layer_norm(values, gain_row):
    centred = values - jnp.mean(values, axis=-1, keepdims=True)
    spread = jnp.mean(centred * centred, axis=-1, keepdims=True)
    return centred * lax.rsqrt(spread + 1e-05) * gain_row


def swish_act(values):
    return values * jax.nn.sigmoid(values)


def neighbour(values, offset):
    if offset > 0:
        filler = jnp.zeros((offset,) + values.shape[1:], values.dtype)
        return jnp.concatenate([values[offset:], filler], axis=0)
    if offset < 0:
        filler = jnp.zeros((-offset,) + values.shape[1:], values.dtype)
        return jnp.concatenate([filler, values[:offset]], axis=0)
    return values


def frame_plan(utter_len, bucket_id):
    position = jnp.arange(FRAMES, dtype=jnp.int32)
    bucket_len = BUCKET * (bucket_id + 1)
    segment = position // bucket_len
    offset_in = position - segment * bucket_len
    slot_index = jnp.arange(SLOTS, dtype=jnp.int32)
    slot_limit = jnp.sum(
        jnp.where(segment[:, None] == slot_index[None, :], utter_len[None, :], 0), axis=1
    )
    is_valid = offset_in < slot_limit
    allowed = (segment[:, None] == segment[None, :]) & is_valid[None, :] | (
        position[:, None] == position[None, :]
    )
    tap_list = []
    for tap_index in range(KERNEL):
        shift_by = tap_index - KERNEL // 2
        same_slot = (neighbour(segment + 1, shift_by) == segment + 1) & neighbour(
            is_valid, shift_by
        )
        tap_list.append(same_slot.astype(jnp.float32))
    return (allowed, jnp.stack(tap_list, axis=0))


def sinusoid(sign):
    column = jnp.arange(D, dtype=jnp.int32)
    rates = jnp.exp((column // 2).astype(jnp.float32) * (-2.0 * math.log(10000.0) / D))
    phase = (column % 2).astype(jnp.float32) * (0.5 * math.pi)
    coarse = sign * (16 * jnp.arange(2 * FRAMES // 16, dtype=jnp.int32) - (FRAMES - 1)).astype(jnp.float32)
    fine = sign * jnp.arange(16, dtype=jnp.int32).astype(jnp.float32)
    angle = coarse[:, None] * rates[None, :]
    rest = fine[:, None] * rates[None, :] + phase[None, :]
    sin_a, cos_a = lax.optimization_barrier((jnp.sin(angle), jnp.cos(angle)))
    sin_b, cos_b = lax.optimization_barrier((jnp.sin(rest), jnp.cos(rest)))
    table = sin_a[:, None] * cos_b[None] + cos_a[:, None] * sin_b[None]
    return table.reshape(2 * FRAMES, D)


def depthwise(values, kernel_rows, tap_masks):
    running = jnp.zeros_like(values)
    for tap_index in range(KERNEL):
        moved = neighbour(values, tap_index - KERNEL // 2)
        running = running + moved * tap_masks[tap_index][:, None] * kernel_rows[tap_index][None, :]
    return running


def conv_inner(gated, gain_inner, kernel_rows, tap_masks):
    gated_out = gated[:, :D] * jax.nn.sigmoid(gated[:, D:])
    return swish_act(layer_norm(depthwise(gated_out, kernel_rows, tap_masks), gain_inner))


def ffn_forward(values, gain_row, weight_in, weight_out):
    normed, norm_pull = jax.vjp(layer_norm, values, gain_row)
    normed_low = normed.astype(jnp.bfloat16)
    hidden = matmul(normed_low, weight_in)
    active = swish_act(hidden).astype(jnp.bfloat16)
    return (matmul(active, weight_out), (norm_pull, normed_low, hidden, active))


def ffn_backward(grad_branch, kept_state, weight_in, weight_out):
    norm_pull, normed_low, hidden, active = kept_state
    grad_out = grad_branch.astype(jnp.bfloat16)
    grad_active = right_product(grad_out, weight_out)
    swish_value, swish_pull = jax.vjp(swish_act, hidden)
    grad_hidden = swish_pull(grad_active)[0].astype(jnp.bfloat16)
    grad_normed = right_product(grad_hidden, weight_in)
    grad_values, grad_gain = norm_pull(grad_normed)
    return (grad_values, grad_gain[None], [(normed_low, grad_hidden)], [(active, grad_out)])


TABLE = 2 * FRAMES
SCALE = HEAD_DIM ** (-0.5)


def nn(left_side, right_side):
    return lax.dot_general(
        left_side, right_side, (((1,), (0,)), ((), ())), preferred_element_type=jnp.float32
    )


def attend_kernel(q_ref, k_ref, v_ref, bias_ref, pos_ref, allow_ref, mixed_ref, prob_ref):
    query = q_ref[...].astype(jnp.float32)
    query_u = ((query + bias_ref[0:1, :]) * SCALE).astype(jnp.bfloat16)
    query_v = ((query + bias_ref[1:2, :]) * SCALE).astype(jnp.bfloat16)
    table = right_product(query_v, pos_ref[...])
    for m in range(MICRO):
        rows = slice(m * FRAMES, (m + 1) * FRAMES)
        content = right_product(query_u[rows], k_ref[rows, :])
        moved = pltpu.roll(table[rows], TABLE - FRAMES + 1, 1, stride=1, stride_axis=0)
        scores = jnp.where(allow_ref[m] > 0, content + moved[:, :FRAMES], -1e30)
        weight = jnp.exp(scores - jnp.max(scores, axis=-1, keepdims=True))
        prob = (weight / jnp.sum(weight, axis=-1, keepdims=True)).astype(jnp.bfloat16)
        prob_ref[m, 0] = prob
        mixed_ref[rows, :] = nn(prob, v_ref[rows, :]).astype(jnp.bfloat16)


def attend_back_kernel(
    q_ref, k_ref, v_ref, bias_ref, pos_ref, prob_ref, grad_ref, dq_ref, dk_ref, dv_ref, dpos_ref, dbias_ref
):
    query = q_ref[...].astype(jnp.float32)
    query_u = ((query + bias_ref[0:1, :]) * SCALE).astype(jnp.bfloat16)
    query_v = ((query + bias_ref[1:2, :]) * SCALE).astype(jnp.bfloat16)
    across = lax.broadcasted_iota(jnp.int32, (FRAMES, FRAMES), 0)
    down = lax.broadcasted_iota(jnp.int32, (FRAMES, FRAMES), 1)
    swap = jnp.where(across + down == FRAMES - 1, 1.0, 0.0).astype(jnp.bfloat16)
    tables, grads_u = [], []
    for m in range(MICRO):
        rows = slice(m * FRAMES, (m + 1) * FRAMES)
        prob = prob_ref[m, 0]
        grad = grad_ref[rows, :]
        dv_ref[rows, :] = left_product(prob, grad).astype(jnp.bfloat16)
        grad_prob = right_product(grad, v_ref[rows, :])
        wide = prob.astype(jnp.float32)
        inner = jnp.sum(wide * grad_prob, axis=-1, keepdims=True)
        grad_score = wide * (grad_prob - inner)
        low = grad_score.astype(jnp.bfloat16)
        grads_u.append(nn(low, k_ref[rows, :]))
        dk_ref[rows, :] = left_product(low, query_u[rows]).astype(jnp.bfloat16)
        turned = nn(low, swap)
        padded = jnp.concatenate([turned, jnp.zeros_like(turned)], axis=1)
        tables.append(pltpu.roll(padded, 0, 1, stride=1, stride_axis=0))
    table = jnp.concatenate(tables, axis=0).astype(jnp.bfloat16)
    grad_u = jnp.concatenate(grads_u, axis=0) * SCALE
    grad_v = nn(table, pos_ref[...]) * SCALE
    dpos_ref[...] = left_product(table, query_v).astype(jnp.bfloat16)
    dq_ref[...] = (grad_u + grad_v).astype(jnp.bfloat16)
    dbias_ref[0:1, :] = jnp.sum(grad_u, axis=0, keepdims=True)
    dbias_ref[1:2, :] = jnp.sum(grad_v, axis=0, keepdims=True)


def head_spec(rows, offset=0):
    return pl.BlockSpec((rows, HEAD_DIM), lambda h: (0, offset + h))


PROB_SPEC = pl.BlockSpec((MICRO, 1, FRAMES, FRAMES), lambda h: (0, h, 0, 0))


def attend(project, bias, positions, allowed):
    rows = project.shape[0]
    return pl.pallas_call(
        attend_kernel,
        grid=(HEADS,),
        out_shape=[
            jax.ShapeDtypeStruct((rows, D), jnp.bfloat16),
            jax.ShapeDtypeStruct((MICRO, HEADS, FRAMES, FRAMES), jnp.bfloat16),
        ],
        in_specs=[
            head_spec(rows),
            head_spec(rows, HEADS),
            head_spec(rows, 2 * HEADS),
            head_spec(2),
            head_spec(TABLE),
            pl.BlockSpec((MICRO, FRAMES, FRAMES), lambda h: (0, 0, 0)),
        ],
        out_specs=[head_spec(rows), PROB_SPEC],
        name="attend",
    )(project, project, project, bias, positions, allowed)


def attend_back(project, bias, positions, prob, grad_mixed):
    rows = project.shape[0]
    wide = jax.ShapeDtypeStruct((rows, D), jnp.bfloat16)
    return pl.pallas_call(
        attend_back_kernel,
        grid=(HEADS,),
        out_shape=[
            wide,
            wide,
            wide,
            jax.ShapeDtypeStruct((TABLE, D), jnp.bfloat16),
            jax.ShapeDtypeStruct((2, D), jnp.float32),
        ],
        in_specs=[
            head_spec(rows),
            head_spec(rows, HEADS),
            head_spec(rows, 2 * HEADS),
            head_spec(2),
            head_spec(TABLE),
            PROB_SPEC,
            head_spec(rows),
        ],
        out_specs=[head_spec(rows), head_spec(rows), head_spec(rows), head_spec(TABLE), head_spec(2)],
        name="attend_back",
    )(project, project, project, bias, positions, prob, grad_mixed)


def attn_forward(values, gain_row, weight_qkv, weight_out, bias, positions, allowed):
    normed, norm_pull = jax.vjp(layer_norm, values, gain_row)
    normed_low = normed.astype(jnp.bfloat16)
    project = matmul(normed_low, weight_qkv).astype(jnp.bfloat16)
    mixed_heads, prob = attend(project, bias, positions, allowed)
    kept_state = (norm_pull, normed_low, project, prob, mixed_heads)
    return (matmul(mixed_heads, weight_out), kept_state)


def attn_backward(grad_res, kept_state, weight_qkv, weight_out, bias, positions):
    norm_pull, normed_low, project, prob, mixed_heads = kept_state
    grad_branch = grad_res.astype(jnp.bfloat16)
    grad_mixed = right_product(grad_branch, weight_out).astype(jnp.bfloat16)
    grad_q, grad_k, grad_v, grad_pos, grad_bias = attend_back(
        project, bias, positions, prob, grad_mixed
    )
    grad_project = jnp.concatenate([grad_q, grad_k, grad_v], axis=1)
    grad_normed = right_product(grad_project, weight_qkv)
    grad_values, grad_gain = norm_pull(grad_normed)
    grad_vec = jnp.concatenate([grad_gain[None], grad_bias], axis=0)
    return (grad_values, grad_vec, [(normed_low, grad_project)], [(mixed_heads, grad_branch)], grad_pos)


def conv_forward(values, gain_row, gain_inner, weight_in, weight_out, kernel_rows, tap_masks):
    normed, norm_pull = jax.vjp(layer_norm, values, gain_row)
    normed_low = normed.astype(jnp.bfloat16)
    gated = matmul(normed_low, weight_in)
    active, inner_pull = jax.vjp(
        partial(conv_inner, tap_masks=tap_masks), gated, gain_inner, kernel_rows
    )
    active_low = active.astype(jnp.bfloat16)
    return (matmul(active_low, weight_out), (norm_pull, normed_low, inner_pull, active_low))


def conv_backward(grad_res, kept_state, weight_in, weight_out):
    norm_pull, normed_low, inner_pull, active_low = kept_state
    grad_branch = grad_res.astype(jnp.bfloat16)
    grad_active = right_product(grad_branch, weight_out)
    grad_gated, grad_inner, grad_taps = inner_pull(grad_active)
    grad_gated_low = grad_gated.astype(jnp.bfloat16)
    grad_normed = right_product(grad_gated_low, weight_in)
    grad_values, grad_gain = norm_pull(grad_normed)
    grad_vec = jnp.concatenate([grad_gain[None], grad_inner[None], grad_taps], axis=0)
    return (grad_values, grad_vec, [(normed_low, grad_gated_low)], [(active_low, grad_branch)])


def other_core(d):
    return d + 1 - 2 * (d % 2)


def flip_x(d):
    return d + 2 - 4 * ((d // 2) % 2)


def flip_y(d):
    return d + 4 - 8 * ((d // 4) % 2)


def greet(peers):
    barrier = pltpu.get_barrier_semaphore()
    for peer in peers:
        pl.semaphore_signal(barrier, inc=1, device_id=peer, device_id_type=MESH)
    pl.semaphore_wait(barrier, len(peers))


def rows_of(start, count):
    return pl.ds(pl.multiple_of(start, 16), count)


ORDER = (0, 1, 2, 4, 6, 7, 3, 5)
DIRECT = (3, 5)


def gather_kernel(n, count, *refs):
    shards = refs[: count + 1]
    fulls = refs[count + 1 : 2 * count + 2]
    send_sem, recv_sem = refs[2 * count + 2 :]
    z = lax.axis_index("fsdp")
    d = lax.axis_index("dp")
    core, place = d % 2, d // 2
    x_peer, y_peer, core_peer = {"dp": flip_x(d)}, {"dp": flip_y(d)}, {"dp": other_core(d)}
    up, down = {"fsdp": (z + 1) % n}, {"fsdp": (z + n - 1) % n}
    greet([up, down, x_peer, y_peer, core_peer])
    used = [0]
    started = []

    def send(src, dst, peer):
        index = used[0]
        used[0] += 1
        copy = pltpu.make_async_remote_copy(
            src_ref=src,
            dst_ref=dst,
            send_sem=send_sem.at[index],
            recv_sem=recv_sem.at[index],
            device_id=peer,
            device_id_type=MESH,
        )
        copy.start()
        started.append(copy)
        return copy

    flip_1 = place + 1 - 2 * (place % 2)
    flip_2 = place + 2 - 4 * (place // 2)

    def span(t, owner):
        depth = shards[t].shape[0]
        if t == count:
            return rows_of(owner * depth, depth)
        if t in DIRECT:
            return rows_of(owner * depth + core * (depth // 2), depth // 2)
        return rows_of(owner * depth + (core * 4 + place) * (depth // 8), depth // 8)

    first = {}

    def launch(t):
        view = shards[t].at[span(t, 0), :]
        first[t, 1] = send(view, fulls[t].at[span(t, z), :], up)
        first[t, 3] = send(view, fulls[t].at[span(t, z), :], down)

    def relay(t):
        view = fulls[t].at[span(t, (z + n - 1) % n), :]
        first[t, 2] = send(view, view, up)

    def piece(t, k, where, half=None):
        depth = shards[t].shape[0]
        part = depth // 8
        start = ((z + n - k) % n) * depth + (core * 4 + where) * part
        if half is None:
            return fulls[t].at[rows_of(start, part), :]
        return fulls[t].at[rows_of(start + half * (part // 2), part // 2), :]

    late = []

    def to_core(t, k):
        depth = shards[t].shape[0]
        half = depth // 2
        view = fulls[t].at[rows_of(((z + n - k) % n) * depth + core * half, half), :]
        late.append(send(view, view, core_peer))

    launch(ORDER[0])
    launch(count)
    launch(ORDER[1])
    for t in [*ORDER, count]:
        depth = shards[t].shape[0]
        late.append(send(shards[t], fulls[t].at[rows_of(z * depth, depth), :], core_peer))
    stages = [(t, k) for t in ORDER if t not in DIRECT for k in (1, 3, 2)]
    across, corner = {}, {}
    for i in range(len(stages) + 2):
        if i < len(stages):
            t, k = stages[i]
            first[t, k].wait_recv()
            if k == 1:
                relay(t)
                following = ORDER.index(t) + 2
                if following < count:
                    launch(ORDER[following])
            mine = piece(t, k, place)
            across[i] = (send(mine, mine, x_peer), send(mine, mine, y_peer))
        if 0 <= i - 1 < len(stages):
            t, k = stages[i - 1]
            by_x, by_y = across[i - 1]
            by_y.wait_recv()
            view = piece(t, k, flip_2, 0)
            one = send(view, view, x_peer)
            by_x.wait_recv()
            view = piece(t, k, flip_1, 1)
            corner[i - 1] = (one, send(view, view, y_peer))
        if 0 <= i - 2 < len(stages):
            for copy in corner[i - 2]:
                copy.wait_recv()
            to_core(*stages[i - 2])
    for t in [*DIRECT, count]:
        first[t, 1].wait_recv()
        relay(t)
    for k in (1, 3, 2):
        for t in DIRECT:
            if k > 1:
                first[t, k].wait_recv()
            to_core(t, k)
    for k in (2, 3):
        first[count, k].wait_recv()
    for copy in late:
        copy.wait_recv()
    for copy in started:
        copy.wait_send()


def gather_all(n, shards, small, collective_id):
    count = len(shards)
    given = list(shards) + [small]
    copies = count * (n - 1) * 6 + n + count
    return pl.pallas_call(
        partial(gather_kernel, n, count),
        out_shape=[jax.ShapeDtypeStruct((n * s.shape[0], s.shape[1]), s.dtype) for s in given],
        in_specs=[pl.BlockSpec(memory_space=pltpu.HBM)] * (count + 1),
        out_specs=[pl.BlockSpec(memory_space=pltpu.HBM)] * (count + 1),
        scratch_shapes=[pltpu.SemaphoreType.DMA((copies,)), pltpu.SemaphoreType.DMA((copies,))],
        compiler_params=pltpu.CompilerParams(collective_id=collective_id, has_side_effects=True),
        name="gather_weights",
    )(*given)


def spread_kernel(count, *refs):
    pieces = refs[:count]
    wholes = refs[count : 2 * count]
    send_sem, recv_sem, own_sem = refs[2 * count :]
    d = lax.axis_index("dp")
    core, place = d % 2, d // 2
    x_peer, y_peer, core_peer = {"dp": flip_x(d)}, {"dp": flip_y(d)}, {"dp": other_core(d)}
    greet([x_peer, y_peer, core_peer])
    used = [0]
    started = []

    def send(src, dst, peer):
        index = used[0]
        used[0] += 1
        copy = pltpu.make_async_remote_copy(
            src_ref=src,
            dst_ref=dst,
            send_sem=send_sem.at[index],
            recv_sem=recv_sem.at[index],
            device_id=peer,
            device_id_type=MESH,
        )
        copy.start()
        started.append(copy)
        return copy

    flip_1 = place + 1 - 2 * (place % 2)
    flip_2 = place + 2 - 4 * (place // 2)

    def region(t, owner_core, where, half=None):
        part = pieces[t].shape[0]
        start = (owner_core * 4 + where) * part
        if half is None:
            return wholes[t].at[rows_of(start, part), :]
        return wholes[t].at[rows_of(start + half * (part // 2), part // 2), :]

    across, own, late = [], [], []
    for t in range(count):
        spot = region(t, core, place)
        across.append((send(pieces[t], spot, x_peer), send(pieces[t], spot, y_peer)))
        late.append(send(pieces[t], spot, core_peer))
        keep = pltpu.make_async_copy(pieces[t], spot, own_sem.at[t])
        keep.start()
        own.append(keep)
    corner = []
    for t in range(count):
        by_x, by_y = across[t]
        by_y.wait_recv()
        view = region(t, core, flip_2, 0)
        one = send(view, view, x_peer)
        view = region(t, core, flip_2)
        late.append(send(view, view, core_peer))
        by_x.wait_recv()
        view = region(t, core, flip_1, 1)
        corner.append((one, send(view, view, y_peer)))
        view = region(t, core, flip_1)
        late.append(send(view, view, core_peer))
    for t in range(count):
        for copy in corner[t]:
            copy.wait_recv()
        view = region(t, core, 3 - place)
        late.append(send(view, view, core_peer))
    for copy in own:
        copy.wait()
    for copy in late:
        copy.wait_recv()
    for copy in started:
        copy.wait_send()


def spread_all(pieces, collective_id):
    count = len(pieces)
    return pl.pallas_call(
        partial(spread_kernel, count),
        out_shape=[jax.ShapeDtypeStruct((8 * s.shape[0], s.shape[1]), s.dtype) for s in pieces],
        in_specs=[pl.BlockSpec(memory_space=pltpu.VMEM)] * count,
        out_specs=[pl.BlockSpec(memory_space=pltpu.HBM)] * count,
        scratch_shapes=[
            pltpu.SemaphoreType.DMA((8 * count,)),
            pltpu.SemaphoreType.DMA((8 * count,)),
            pltpu.SemaphoreType.DMA((count,)),
        ],
        compiler_params=pltpu.CompilerParams(collective_id=collective_id, has_side_effects=True),
        name="spread_sums",
    )(*pieces)


def add_rows(dst, dst_row, src, src_row, count):
    @pl.loop(0, count // 16)
    def _(step):
        at = pl.ds(pl.multiple_of(dst_row + step * 16, 16), 16)
        take = pl.ds(pl.multiple_of(src_row + step * 16, 16), 16)
        total = dst[at, :].astype(jnp.float32) + src[take, :].astype(jnp.float32)
        dst[at, :] = total.astype(jnp.bfloat16)


def sums_kernel(n, plan, small, *refs):
    count = len(plan)
    inputs = sum(2 * len(widths) for _, widths in plan)
    operands = list(refs[:inputs])
    refs = refs[inputs:]
    if small:
        small_ref, refs = refs[0], refs[1:]
    outs, refs = refs[:count], refs[count:]
    if small:
        small_out, refs = refs[0], refs[1:]
    held, refs = refs[:count], refs[count:]
    from_core, refs = refs[:count], refs[count:]
    from_first, refs = refs[:count], refs[count:]
    from_second, refs = refs[:count], refs[count:]
    from_z, refs = refs[:count], refs[count:]
    if small:
        (small_held, small_got, small_z), refs = refs[:3], refs[3:]
    send_sem, recv_sem = refs
    pairs = []
    for _, widths in plan:
        pairs.append([(operands.pop(0), operands.pop(0)) for _ in widths])
    z = lax.axis_index("fsdp")
    d = lax.axis_index("dp")
    core, place = d % 2, d // 2
    x_bit, y_bit = place % 2, place // 2
    peers = [{"dp": flip_x(d)}, {"dp": flip_y(d)}]
    core_peer = {"dp": other_core(d)}
    z_peers = [{"fsdp": (z + k) % n} for k in range(1, n)]
    greet(z_peers + peers + [core_peer])
    used = [0]
    started = []

    def send(src, dst, peer, keep=True):
        index = used[0]
        used[0] += 1
        copy = pltpu.make_async_remote_copy(
            src_ref=src,
            dst_ref=dst,
            send_sem=send_sem.at[index],
            recv_sem=recv_sem.at[index],
            device_id=peer,
            device_id_type=MESH,
        )
        copy.start()
        if keep:
            started.append(copy)
        return copy

    units = [(t, k) for t in range(count) for k in [*range(1, n), 0]]
    part = [rows // (8 * n) for rows, _ in plan]
    arrive, first, second, third = {}, {}, {}, {}

    def make(t, k, spare):
        half = 4 * part[t]
        tile = 128 * 1024 // half
        column = ((z + k) % n) * 2 * half
        offset = 0
        for (left, right), width in zip(pairs[t], plan[t][1]):
            tiles = width // tile

            @pl.loop(0, 2 * tiles)
            def _(step):
                own, index = step // tiles, step % tiles
                side = own * core + (1 - own) * (1 - core)
                source = pl.ds(pl.multiple_of(column + side * half, 128), half)
                row = own * (k * half) + (1 - own) * ((n + spare) * half)
                across = pl.ds(pl.multiple_of(index * tile, 128), tile)
                target = pl.ds(pl.multiple_of(offset + index * tile, 128), tile)
                block = left_product(left[:, source], right[:, across])
                held[t][rows_of(row, half), target] = block.astype(jnp.bfloat16)

            offset += width

    for i in range(len(units) + 6):
        if i < len(units):
            t, k = units[i]
            half, spare = 4 * part[t], i % 2
            if i >= 2 and units[i - 2][0] == t:
                arrive[i - 2].wait_send()
            make(t, k, spare)
            arrive[i] = send(
                held[t].at[pl.ds((n + spare) * half, half), :],
                from_core[t].at[pl.ds(k * half, half), :],
                core_peer,
                keep=i + 2 >= len(units) or units[i + 2][0] != t,
            )
        if small and i < 3:
            if i == 0:
                small_held[...] = small_ref[...]
            else:
                small_copy.wait()
                small_held[...] += small_got[i - 1]
            small_copy = send(small_held, small_got.at[i], [core_peer, *peers][i], keep=False)
        if small and i == 3:
            small_copy.wait()
            small_held[...] += small_got[2]
            width = small_out.shape[1]
            small_z_copies = [
                send(
                    small_held.at[:, pl.ds(pl.multiple_of(((z + k) % n) * width, 128), width)],
                    small_z.at[k - 1],
                    z_peers[k - 1],
                )
                for k in range(1, n)
            ]
        j = i - 1
        if 0 <= j < len(units):
            t, k = units[j]
            p, base = part[t], k * 4 * part[t]
            arrive[j].wait_recv()
            add_rows(held[t], base, from_core[t], base, 4 * p)
            if j % 2 == 0:
                first[j] = [
                    send(
                        held[t].at[rows_of(base + (2 * y + 1 - x_bit) * p, p), :],
                        from_first[t].at[pl.ds((2 * k + y) * p, p), :],
                        peers[0],
                    )
                    for y in range(2)
                ]
            else:
                first[j] = [
                    send(
                        held[t].at[rows_of(base + 2 * (1 - y_bit) * p, 2 * p), :],
                        from_first[t].at[pl.ds(2 * k * p, 2 * p), :],
                        peers[1],
                    )
                ]
        j = i - 3
        if 0 <= j < len(units):
            t, k = units[j]
            p, base = part[t], k * 4 * part[t]
            for copy in first[j]:
                copy.wait_recv()
            if j % 2 == 0:
                for y in range(2):
                    add_rows(held[t], base + (2 * y + x_bit) * p, from_first[t], (2 * k + y) * p, p)
                gone, peer = base + (2 * (1 - y_bit) + x_bit) * p, peers[1]
            else:
                add_rows(held[t], base + 2 * y_bit * p, from_first[t], 2 * k * p, 2 * p)
                gone, peer = base + (2 * y_bit + 1 - x_bit) * p, peers[0]
            second[j] = send(held[t].at[rows_of(gone, p), :], from_second[t].at[pl.ds(k * p, p), :], peer)
        j = i - 5
        if 0 <= j < len(units):
            t, k = units[j]
            p, base = part[t], k * 4 * part[t]
            second[j].wait_recv()
            add_rows(held[t], base + place * p, from_second[t], k * p, p)
            if k > 0:
                third[t, k] = send(
                    held[t].at[rows_of(base + place * p, p), :],
                    from_z[t].at[pl.ds((k - 1) * p, p), :],
                    z_peers[k - 1],
                )
    for t in range(count):
        p = part[t]
        for k in range(1, n):
            third[t, k].wait_recv()

        @pl.loop(0, p // 16)
        def _(step):
            total = held[t][pl.ds(pl.multiple_of(place * p + step * 16, 16), 16), :].astype(jnp.float32)
            for k in range(1, n):
                at = pl.ds(pl.multiple_of((k - 1) * p + step * 16, 16), 16)
                total = total + from_z[t][at, :].astype(jnp.float32)
            outs[t][pl.ds(pl.multiple_of(step * 16, 16), 16), :] = total.astype(jnp.bfloat16)

    if small:
        for copy in small_z_copies:
            copy.wait_recv()
        total = small_held[:, pl.ds(pl.multiple_of(z * width, 128), width)]
        for k in range(1, n):
            total = total + small_z[k - 1]
        small_out[...] = total
    for copy in started:
        copy.wait_send()


def sum_products(n, tensors, small, collective_id):
    plan = [
        (pairs[0][0].shape[1], tuple(right.shape[1] for _, right in pairs)) for pairs in tensors
    ]
    count = len(plan)
    operands = [side for pairs in tensors for pair in pairs for side in pair]
    shapes = [(rows, sum(widths)) for rows, widths in plan]
    out_shape = [jax.ShapeDtypeStruct((r // (8 * n), c), jnp.bfloat16) for r, c in shapes]

    def room(over, under):
        return [pltpu.VMEM((r * over // under, c), jnp.bfloat16) for r, c in shapes]

    scratch = [
        *room(n + 2, 2 * n),
        *room(1, 2),
        *room(1, 4),
        *room(1, 8),
        *room(n - 1, 8 * n),
    ]
    copies = count * (5 * n - 1)
    if small is not None:
        operands.append(small)
        depth, width = small.shape
        out_shape.append(jax.ShapeDtypeStruct((depth, width // n), jnp.float32))
        scratch += [
            pltpu.VMEM((depth, width), jnp.float32),
            pltpu.VMEM((3, depth, width), jnp.float32),
            pltpu.VMEM((n - 1, depth, width // n), jnp.float32),
        ]
        copies += 3 + n - 1
    whole = pl.BlockSpec(memory_space=pltpu.VMEM)
    return pl.pallas_call(
        partial(sums_kernel, n, plan, small is not None),
        out_shape=out_shape,
        in_specs=[whole] * len(operands),
        out_specs=[whole] * len(out_shape),
        scratch_shapes=[
            *scratch,
            pltpu.SemaphoreType.DMA((copies,)),
            pltpu.SemaphoreType.DMA((copies,)),
        ],
        compiler_params=pltpu.CompilerParams(
            collective_id=collective_id, has_side_effects=True, vmem_limit_bytes=63 * 1024 * 1024
        ),
        name="sum_products",
    )(*operands)


EARLY = (6, 7, 4, 5)
LATE = (2, 0, 1, 3)


def fallback_reduce(pairs):
    grad = jnp.concatenate([left_product(left, right) for left, right in pairs], axis=1)
    part = lax.psum_scatter(grad.astype(jnp.bfloat16), "fsdp", scatter_dimension=0, tiled=True)
    return lax.psum(part, "dp")


def on_device(
    fast,
    n,
    inputs,
    cotangent,
    lengths,
    buckets,
    ffn1_in,
    ffn1_out,
    attn_in,
    attn_out,
    conv_in,
    conv_out,
    ffn2_in,
    ffn2_out,
    norm_gains,
    pos_bias,
    kernel,
):
    shards = [ffn1_in, ffn1_out, attn_in, attn_out, conv_in, conv_out, ffn2_in, ffn2_out]
    width = norm_gains.shape[1]
    vectors = jnp.concatenate(
        [norm_gains, pos_bias, kernel, jnp.zeros((3, width), norm_gains.dtype)], axis=0
    )
    if fast:
        gathered = gather_all(n, shards, vectors, 0)
        weights, vec = gathered[:8], gathered[8]
        vec = vec.reshape(n, 16, width).transpose(1, 0, 2).reshape(16, D)
    else:
        weights = [lax.all_gather(s, "fsdp", axis=0, tiled=True) for s in shards]
        vec = lax.all_gather(vectors, "fsdp", axis=1, tiled=True)
    vec = vec.astype(jnp.float32)
    gains, biases, taps = vec[0:6], vec[6:8], vec[8:13]
    plans = [frame_plan(lengths[m], buckets[m]) for m in range(MICRO)]
    allowed = jnp.stack([p[0] for p in plans], axis=0).astype(jnp.float32)
    tap_masks = jnp.concatenate([p[1] for p in plans], axis=1)
    table_low = sinusoid(1).astype(jnp.bfloat16)
    mirror_low = sinusoid(-1).astype(jnp.bfloat16)

    stream = inputs.astype(jnp.float32)
    branch, kept_one = ffn_forward(stream, gains[0], weights[0], weights[1])
    section_one = stream + 0.5 * branch
    positions = matmul(table_low, weights[2][:, 3 * D :]).astype(jnp.bfloat16)
    mirrored = matmul(mirror_low, weights[2][:, 3 * D :]).astype(jnp.bfloat16)
    weight_qkv = weights[2][:, : 3 * D]
    branch, kept_two = attn_forward(
        section_one, gains[1], weight_qkv, weights[3], biases, positions, allowed
    )
    section_two = section_one + branch
    branch, kept_three = conv_forward(
        section_two, gains[2], gains[3], weights[4], weights[5], taps, tap_masks
    )
    section_three = section_two + branch
    branch, kept_four = ffn_forward(section_three, gains[4], weights[6], weights[7])
    section_four = section_three + 0.5 * branch
    final_out, final_pull = jax.vjp(layer_norm, section_four, gains[5])
    grad_stream, grad_final = final_pull(cotangent.astype(jnp.float32))

    grad_values, grad_vec4, grad_in4, grad_out4 = ffn_backward(
        0.5 * grad_stream, kept_four, weights[6], weights[7]
    )
    sums = [None] * 8
    grad_stream = grad_stream + grad_values
    grad_values, grad_vec3, grad_in3, grad_out3 = conv_backward(
        grad_stream, kept_three, weights[4], weights[5]
    )
    grad_stream = grad_stream + grad_values
    grad_values, grad_vec2, grad_in2, grad_out2, grad_pos = attn_backward(
        grad_stream, kept_two, weight_qkv, weights[3], biases, mirrored
    )
    grad_stream = grad_stream + grad_values
    grad_values, grad_vec1, grad_in1, grad_out1 = ffn_backward(
        0.5 * grad_stream, kept_one, weights[0], weights[1]
    )
    grad_in2 = grad_in2 + [(mirror_low, grad_pos)]
    grad_stream = grad_stream + grad_values

    grad_vectors = jnp.concatenate(
        [
            grad_vec1,
            grad_vec2[0:1],
            grad_vec3[0:2],
            grad_vec4,
            grad_final[None],
            grad_vec2[1:3],
            grad_vec3[2:7],
            jnp.zeros((3, D), jnp.float32),
        ],
        axis=0,
    )
    tensors = [grad_in1, grad_out1, grad_in2, grad_out2, grad_in3, grad_out3, grad_in4, grad_out4]
    if fast:
        early = sum_products(n, [tensors[i] for i in EARLY], None, 2)
        *late, grad_small = sum_products(n, [tensors[i] for i in LATE], grad_vectors, 3)
        for index, total in zip(EARLY + LATE, list(early) + late):
            sums[index] = total
        sums = spread_all(sums, 1)
    else:
        sums = [fallback_reduce(pairs) for pairs in tensors]
        grad_small = lax.psum(
            lax.psum_scatter(grad_vectors, "fsdp", scatter_dimension=1, tiled=True), "dp"
        )
    grads = [s.astype(jnp.float32) for s in sums]
    return (
        final_out.astype(jnp.bfloat16),
        grad_stream,
        *grads,
        grad_small[0:6],
        grad_small[6:8],
        grad_small[8:13],
    )


def solution(mesh):
    in_specs = (
        P(("dp", "fsdp"), None),
        P(("dp", "fsdp"), None),
        P(("dp", "fsdp"), None),
        P(("dp", "fsdp")),
        P("fsdp", None),
        P("fsdp", None),
        P("fsdp", None),
        P("fsdp", None),
        P("fsdp", None),
        P("fsdp", None),
        P("fsdp", None),
        P("fsdp", None),
        P(None, "fsdp"),
        P(None, "fsdp"),
        P(None, "fsdp"),
    )
    out_specs = (
        P(("dp", "fsdp"), None),
        P(("dp", "fsdp"), None),
        P("fsdp", None),
        P("fsdp", None),
        P("fsdp", None),
        P("fsdp", None),
        P("fsdp", None),
        P("fsdp", None),
        P("fsdp", None),
        P("fsdp", None),
        P(None, "fsdp"),
        P(None, "fsdp"),
        P(None, "fsdp"),
    )
    sizes = dict(mesh.shape)
    n = sizes["fsdp"]
    fast = sizes["dp"] == 8 and n == 4
    return jax.shard_map(
        partial(on_device, fast, n), mesh=mesh, in_specs=in_specs, out_specs=out_specs, check_vma=False
    )
```

```python
from functools import partial
import math

import jax
import jax.numpy as jnp
from jax import lax
from jax.experimental import pallas as pl
from jax.experimental.pallas import tpu as pltpu
from jax.sharding import PartitionSpec as P

MESH = pl.DeviceIdType.MESH

D = 1024
HEADS = 8
HEAD_DIM = 128
KERNEL = 5
BUCKET = 64
MICRO = 2
FRAMES = 192
SLOTS = 3


def matmul(left_side, right_side):
    return jnp.dot(left_side, right_side, preferred_element_type=jnp.float32)


def left_product(left_side, right_side):
    return lax.dot_general(
        left_side, right_side, (((0,), (0,)), ((), ())), preferred_element_type=jnp.float32
    )


def right_product(left_side, right_side):
    return lax.dot_general(
        left_side, right_side, (((1,), (1,)), ((), ())), preferred_element_type=jnp.float32
    )


def layer_norm(values, gain_row):
    centred = values - jnp.mean(values, axis=-1, keepdims=True)
    spread = jnp.mean(centred * centred, axis=-1, keepdims=True)
    return centred * lax.rsqrt(spread + 1e-05) * gain_row


def swish_act(values):
    return values * jax.nn.sigmoid(values)


def neighbour(values, offset):
    if offset > 0:
        filler = jnp.zeros((offset,) + values.shape[1:], values.dtype)
        return jnp.concatenate([values[offset:], filler], axis=0)
    if offset < 0:
        filler = jnp.zeros((-offset,) + values.shape[1:], values.dtype)
        return jnp.concatenate([filler, values[:offset]], axis=0)
    return values


def frame_plan(utter_len, bucket_id):
    position = jnp.arange(FRAMES, dtype=jnp.int32)
    bucket_len = BUCKET * (bucket_id + 1)
    segment = position // bucket_len
    offset_in = position - segment * bucket_len
    slot_index = jnp.arange(SLOTS, dtype=jnp.int32)
    slot_limit = jnp.sum(
        jnp.where(segment[:, None] == slot_index[None, :], utter_len[None, :], 0), axis=1
    )
    is_valid = offset_in < slot_limit
    allowed = (segment[:, None] == segment[None, :]) & is_valid[None, :] | (
        position[:, None] == position[None, :]
    )
    tap_list = []
    for tap_index in range(KERNEL):
        shift_by = tap_index - KERNEL // 2
        same_slot = (neighbour(segment + 1, shift_by) == segment + 1) & neighbour(
            is_valid, shift_by
        )
        tap_list.append(same_slot.astype(jnp.float32))
    return (allowed, jnp.stack(tap_list, axis=0))


def sinusoid(sign):
    column = jnp.arange(D, dtype=jnp.int32)
    rates = jnp.exp((column // 2).astype(jnp.float32) * (-2.0 * math.log(10000.0) / D))
    phase = (column % 2).astype(jnp.float32) * (0.5 * math.pi)
    coarse = sign * (16 * jnp.arange(2 * FRAMES // 16, dtype=jnp.int32) - (FRAMES - 1)).astype(jnp.float32)
    fine = sign * jnp.arange(16, dtype=jnp.int32).astype(jnp.float32)
    angle = coarse[:, None] * rates[None, :]
    rest = fine[:, None] * rates[None, :] + phase[None, :]
    sin_a, cos_a = lax.optimization_barrier((jnp.sin(angle), jnp.cos(angle)))
    sin_b, cos_b = lax.optimization_barrier((jnp.sin(rest), jnp.cos(rest)))
    table = sin_a[:, None] * cos_b[None] + cos_a[:, None] * sin_b[None]
    return table.reshape(2 * FRAMES, D)


def depthwise(values, kernel_rows, tap_masks):
    running = jnp.zeros_like(values)
    for tap_index in range(KERNEL):
        moved = neighbour(values, tap_index - KERNEL // 2)
        running = running + moved * tap_masks[tap_index][:, None] * kernel_rows[tap_index][None, :]
    return running


def conv_inner(gated, gain_inner, kernel_rows, tap_masks):
    gated_out = gated[:, :D] * jax.nn.sigmoid(gated[:, D:])
    return swish_act(layer_norm(depthwise(gated_out, kernel_rows, tap_masks), gain_inner))


def ffn_forward(values, gain_row, weight_in, weight_out):
    normed, norm_pull = jax.vjp(layer_norm, values, gain_row)
    normed_low = normed.astype(jnp.bfloat16)
    hidden = matmul(normed_low, weight_in)
    active = swish_act(hidden).astype(jnp.bfloat16)
    return (matmul(active, weight_out), (norm_pull, normed_low, hidden, active))


def ffn_backward(grad_branch, kept_state, weight_in, weight_out):
    norm_pull, normed_low, hidden, active = kept_state
    grad_out = grad_branch.astype(jnp.bfloat16)
    grad_active = right_product(grad_out, weight_out)
    swish_value, swish_pull = jax.vjp(swish_act, hidden)
    grad_hidden = swish_pull(grad_active)[0].astype(jnp.bfloat16)
    grad_normed = right_product(grad_hidden, weight_in)
    grad_values, grad_gain = norm_pull(grad_normed)
    return (grad_values, grad_gain[None], [(normed_low, grad_hidden)], [(active, grad_out)])


TABLE = 2 * FRAMES
SCALE = HEAD_DIM ** (-0.5)


def nn(left_side, right_side):
    return lax.dot_general(
        left_side, right_side, (((1,), (0,)), ((), ())), preferred_element_type=jnp.float32
    )


def attend_kernel(q_ref, k_ref, v_ref, bias_ref, pos_ref, allow_ref, mixed_ref, prob_ref):
    query = q_ref[...].astype(jnp.float32)
    query_u = ((query + bias_ref[0:1, :]) * SCALE).astype(jnp.bfloat16)
    query_v = ((query + bias_ref[1:2, :]) * SCALE).astype(jnp.bfloat16)
    table = right_product(query_v, pos_ref[...])
    for m in range(MICRO):
        rows = slice(m * FRAMES, (m + 1) * FRAMES)
        content = right_product(query_u[rows], k_ref[rows, :])
        moved = pltpu.roll(table[rows], TABLE - FRAMES + 1, 1, stride=1, stride_axis=0)
        scores = jnp.where(allow_ref[m] > 0, content + moved[:, :FRAMES], -1e30)
        weight = jnp.exp(scores - jnp.max(scores, axis=-1, keepdims=True))
        prob = (weight / jnp.sum(weight, axis=-1, keepdims=True)).astype(jnp.bfloat16)
        prob_ref[m, 0] = prob
        mixed_ref[rows, :] = nn(prob, v_ref[rows, :]).astype(jnp.bfloat16)


def attend_back_kernel(
    q_ref, k_ref, v_ref, bias_ref, pos_ref, prob_ref, grad_ref, dq_ref, dk_ref, dv_ref, dpos_ref, dbias_ref
):
    query = q_ref[...].astype(jnp.float32)
    query_u = ((query + bias_ref[0:1, :]) * SCALE).astype(jnp.bfloat16)
    query_v = ((query + bias_ref[1:2, :]) * SCALE).astype(jnp.bfloat16)
    across = lax.broadcasted_iota(jnp.int32, (FRAMES, FRAMES), 0)
    down = lax.broadcasted_iota(jnp.int32, (FRAMES, FRAMES), 1)
    swap = jnp.where(across + down == FRAMES - 1, 1.0, 0.0).astype(jnp.bfloat16)
    tables, grads_u = [], []
    for m in range(MICRO):
        rows = slice(m * FRAMES, (m + 1) * FRAMES)
        prob = prob_ref[m, 0]
        grad = grad_ref[rows, :]
        dv_ref[rows, :] = left_product(prob, grad).astype(jnp.bfloat16)
        grad_prob = right_product(grad, v_ref[rows, :])
        wide = prob.astype(jnp.float32)
        inner = jnp.sum(wide * grad_prob, axis=-1, keepdims=True)
        grad_score = wide * (grad_prob - inner)
        low = grad_score.astype(jnp.bfloat16)
        grads_u.append(nn(low, k_ref[rows, :]))
        dk_ref[rows, :] = left_product(low, query_u[rows]).astype(jnp.bfloat16)
        turned = nn(low, swap)
        padded = jnp.concatenate([turned, jnp.zeros_like(turned)], axis=1)
        tables.append(pltpu.roll(padded, 0, 1, stride=1, stride_axis=0))
    table = jnp.concatenate(tables, axis=0).astype(jnp.bfloat16)
    grad_u = jnp.concatenate(grads_u, axis=0) * SCALE
    grad_v = nn(table, pos_ref[...]) * SCALE
    dpos_ref[...] = left_product(table, query_v).astype(jnp.bfloat16)
    dq_ref[...] = (grad_u + grad_v).astype(jnp.bfloat16)
    dbias_ref[0:1, :] = jnp.sum(grad_u, axis=0, keepdims=True)
    dbias_ref[1:2, :] = jnp.sum(grad_v, axis=0, keepdims=True)


def head_spec(rows, offset=0):
    return pl.BlockSpec((rows, HEAD_DIM), lambda h: (0, offset + h))


PROB_SPEC = pl.BlockSpec((MICRO, 1, FRAMES, FRAMES), lambda h: (0, h, 0, 0))


def attend(project, bias, positions, allowed):
    rows = project.shape[0]
    return pl.pallas_call(
        attend_kernel,
        grid=(HEADS,),
        out_shape=[
            jax.ShapeDtypeStruct((rows, D), jnp.bfloat16),
            jax.ShapeDtypeStruct((MICRO, HEADS, FRAMES, FRAMES), jnp.bfloat16),
        ],
        in_specs=[
            head_spec(rows),
            head_spec(rows, HEADS),
            head_spec(rows, 2 * HEADS),
            head_spec(2),
            head_spec(TABLE),
            pl.BlockSpec((MICRO, FRAMES, FRAMES), lambda h: (0, 0, 0)),
        ],
        out_specs=[head_spec(rows), PROB_SPEC],
        name="attend",
    )(project, project, project, bias, positions, allowed)


def attend_back(project, bias, positions, prob, grad_mixed):
    rows = project.shape[0]
    wide = jax.ShapeDtypeStruct((rows, D), jnp.bfloat16)
    return pl.pallas_call(
        attend_back_kernel,
        grid=(HEADS,),
        out_shape=[
            wide,
            wide,
            wide,
            jax.ShapeDtypeStruct((TABLE, D), jnp.bfloat16),
            jax.ShapeDtypeStruct((2, D), jnp.float32),
        ],
        in_specs=[
            head_spec(rows),
            head_spec(rows, HEADS),
            head_spec(rows, 2 * HEADS),
            head_spec(2),
            head_spec(TABLE),
            PROB_SPEC,
            head_spec(rows),
        ],
        out_specs=[head_spec(rows), head_spec(rows), head_spec(rows), head_spec(TABLE), head_spec(2)],
        name="attend_back",
    )(project, project, project, bias, positions, prob, grad_mixed)


def attn_forward(values, gain_row, weight_qkv, weight_out, bias, positions, allowed):
    normed, norm_pull = jax.vjp(layer_norm, values, gain_row)
    normed_low = normed.astype(jnp.bfloat16)
    project = matmul(normed_low, weight_qkv).astype(jnp.bfloat16)
    mixed_heads, prob = attend(project, bias, positions, allowed)
    kept_state = (norm_pull, normed_low, project, prob, mixed_heads)
    return (matmul(mixed_heads, weight_out), kept_state)


def attn_backward(grad_res, kept_state, weight_qkv, weight_out, bias, positions):
    norm_pull, normed_low, project, prob, mixed_heads = kept_state
    grad_branch = grad_res.astype(jnp.bfloat16)
    grad_mixed = right_product(grad_branch, weight_out).astype(jnp.bfloat16)
    grad_q, grad_k, grad_v, grad_pos, grad_bias = attend_back(
        project, bias, positions, prob, grad_mixed
    )
    grad_project = jnp.concatenate([grad_q, grad_k, grad_v], axis=1)
    grad_normed = right_product(grad_project, weight_qkv)
    grad_values, grad_gain = norm_pull(grad_normed)
    grad_vec = jnp.concatenate([grad_gain[None], grad_bias], axis=0)
    return (grad_values, grad_vec, [(normed_low, grad_project)], [(mixed_heads, grad_branch)], grad_pos)


def conv_forward(values, gain_row, gain_inner, weight_in, weight_out, kernel_rows, tap_masks):
    normed, norm_pull = jax.vjp(layer_norm, values, gain_row)
    normed_low = normed.astype(jnp.bfloat16)
    gated = matmul(normed_low, weight_in)
    active, inner_pull = jax.vjp(
        partial(conv_inner, tap_masks=tap_masks), gated, gain_inner, kernel_rows
    )
    active_low = active.astype(jnp.bfloat16)
    return (matmul(active_low, weight_out), (norm_pull, normed_low, inner_pull, active_low))


def conv_backward(grad_res, kept_state, weight_in, weight_out):
    norm_pull, normed_low, inner_pull, active_low = kept_state
    grad_branch = grad_res.astype(jnp.bfloat16)
    grad_active = right_product(grad_branch, weight_out)
    grad_gated, grad_inner, grad_taps = inner_pull(grad_active)
    grad_gated_low = grad_gated.astype(jnp.bfloat16)
    grad_normed = right_product(grad_gated_low, weight_in)
    grad_values, grad_gain = norm_pull(grad_normed)
    grad_vec = jnp.concatenate([grad_gain[None], grad_inner[None], grad_taps], axis=0)
    return (grad_values, grad_vec, [(normed_low, grad_gated_low)], [(active_low, grad_branch)])


def other_core(d):
    return d + 1 - 2 * (d % 2)


def flip_x(d):
    return d + 2 - 4 * ((d // 2) % 2)


def flip_y(d):
    return d + 4 - 8 * ((d // 4) % 2)


def greet(peers):
    barrier = pltpu.get_barrier_semaphore()
    for peer in peers:
        pl.semaphore_signal(barrier, inc=1, device_id=peer, device_id_type=MESH)
    pl.semaphore_wait(barrier, len(peers))


def rows_of(start, count):
    return pl.ds(pl.multiple_of(start, 16), count)


ORDER = (0, 1, 2, 4, 6, 7, 3, 5)
DIRECT = (3, 5)


def gather_kernel(n, count, *refs):
    shards = refs[: count + 1]
    fulls = refs[count + 1 : 2 * count + 2]
    send_sem, recv_sem = refs[2 * count + 2 :]
    z = lax.axis_index("fsdp")
    d = lax.axis_index("dp")
    core, place = d % 2, d // 2
    x_peer, y_peer, core_peer = {"dp": flip_x(d)}, {"dp": flip_y(d)}, {"dp": other_core(d)}
    up, down = {"fsdp": (z + 1) % n}, {"fsdp": (z + n - 1) % n}
    greet([up, down, x_peer, y_peer, core_peer])
    used = [0]
    started = []

    def send(src, dst, peer):
        index = used[0]
        used[0] += 1
        copy = pltpu.make_async_remote_copy(
            src_ref=src,
            dst_ref=dst,
            send_sem=send_sem.at[index],
            recv_sem=recv_sem.at[index],
            device_id=peer,
            device_id_type=MESH,
        )
        copy.start()
        started.append(copy)
        return copy

    flip_1 = place + 1 - 2 * (place % 2)
    flip_2 = place + 2 - 4 * (place // 2)

    def span(t, owner):
        depth = shards[t].shape[0]
        if t == count:
            return rows_of(owner * depth, depth)
        if t in DIRECT:
            return rows_of(owner * depth + core * (depth // 2), depth // 2)
        return rows_of(owner * depth + (core * 4 + place) * (depth // 8), depth // 8)

    first = {}

    def launch(t):
        view = shards[t].at[span(t, 0), :]
        first[t, 1] = send(view, fulls[t].at[span(t, z), :], up)
        first[t, 3] = send(view, fulls[t].at[span(t, z), :], down)

    def relay(t):
        view = fulls[t].at[span(t, (z + n - 1) % n), :]
        first[t, 2] = send(view, view, up)

    def piece(t, k, where, half=None):
        depth = shards[t].shape[0]
        part = depth // 8
        start = ((z + n - k) % n) * depth + (core * 4 + where) * part
        if half is None:
            return fulls[t].at[rows_of(start, part), :]
        return fulls[t].at[rows_of(start + half * (part // 2), part // 2), :]

    late = []

    def to_core(t, k):
        depth = shards[t].shape[0]
        half = depth // 2
        view = fulls[t].at[rows_of(((z + n - k) % n) * depth + core * half, half), :]
        late.append(send(view, view, core_peer))

    launch(ORDER[0])
    launch(count)
    launch(ORDER[1])
    for t in [*ORDER, count]:
        depth = shards[t].shape[0]
        late.append(send(shards[t], fulls[t].at[rows_of(z * depth, depth), :], core_peer))
    stages = [(t, k) for t in ORDER if t not in DIRECT for k in (1, 3, 2)]
    across, corner = {}, {}
    for i in range(len(stages) + 2):
        if i < len(stages):
            t, k = stages[i]
            first[t, k].wait_recv()
            if k == 1:
                relay(t)
                following = ORDER.index(t) + 2
                if following < count:
                    launch(ORDER[following])
            mine = piece(t, k, place)
            across[i] = (send(mine, mine, x_peer), send(mine, mine, y_peer))
        if 0 <= i - 1 < len(stages):
            t, k = stages[i - 1]
            by_x, by_y = across[i - 1]
            by_y.wait_recv()
            view = piece(t, k, flip_2, 0)
            one = send(view, view, x_peer)
            by_x.wait_recv()
            view = piece(t, k, flip_1, 1)
            corner[i - 1] = (one, send(view, view, y_peer))
        if 0 <= i - 2 < len(stages):
            for copy in corner[i - 2]:
                copy.wait_recv()
            to_core(*stages[i - 2])
    for t in [*DIRECT, count]:
        first[t, 1].wait_recv()
        relay(t)
    for k in (1, 3, 2):
        for t in DIRECT:
            if k > 1:
                first[t, k].wait_recv()
            to_core(t, k)
    for k in (2, 3):
        first[count, k].wait_recv()
    for copy in late:
        copy.wait_recv()
    for copy in started:
        copy.wait_send()


def gather_all(n, shards, small, collective_id):
    count = len(shards)
    given = list(shards) + [small]
    copies = count * (n - 1) * 6 + n + count
    return pl.pallas_call(
        partial(gather_kernel, n, count),
        out_shape=[jax.ShapeDtypeStruct((n * s.shape[0], s.shape[1]), s.dtype) for s in given],
        in_specs=[pl.BlockSpec(memory_space=pltpu.HBM)] * (count + 1),
        out_specs=[pl.BlockSpec(memory_space=pltpu.HBM)] * (count + 1),
        scratch_shapes=[pltpu.SemaphoreType.DMA((copies,)), pltpu.SemaphoreType.DMA((copies,))],
        compiler_params=pltpu.CompilerParams(collective_id=collective_id, has_side_effects=True),
        name="gather_weights",
    )(*given)


def add_rows(dst, dst_row, src, src_row, count):
    @pl.loop(0, count // 16)
    def _(step):
        at = pl.ds(pl.multiple_of(dst_row + step * 16, 16), 16)
        take = pl.ds(pl.multiple_of(src_row + step * 16, 16), 16)
        total = dst[at, :].astype(jnp.float32) + src[take, :].astype(jnp.float32)
        dst[at, :] = total.astype(jnp.bfloat16)


def sums_kernel(n, plan, extra, *refs):
    small = extra > 0
    count = len(plan)
    inputs = sum(2 * len(widths) for _, widths in plan)
    operands = list(refs[:inputs])
    refs = refs[inputs:]
    if small:
        small_ref, refs = refs[0], refs[1:]
        ready, refs = list(refs[:extra]), refs[extra:]
        wholes, refs = refs[: extra + count], refs[extra + count :]
        small_out, refs = refs[0], refs[1:]
        outs, refs = refs[:count], refs[count:]
    else:
        outs, refs = refs[:count], refs[count:]
    held, refs = refs[:count], refs[count:]
    from_core, refs = refs[:count], refs[count:]
    from_first, refs = refs[:count], refs[count:]
    from_second, refs = refs[:count], refs[count:]
    from_z, refs = refs[:count], refs[count:]
    if small:
        (small_held, small_got, small_z, own_sem), refs = refs[:4], refs[4:]
        ready += list(outs)
    send_sem, recv_sem = refs
    pairs = []
    for _, widths in plan:
        pairs.append([(operands.pop(0), operands.pop(0)) for _ in widths])
    z = lax.axis_index("fsdp")
    d = lax.axis_index("dp")
    core, place = d % 2, d // 2
    x_bit, y_bit = place % 2, place // 2
    peers = [{"dp": flip_x(d)}, {"dp": flip_y(d)}]
    core_peer = {"dp": other_core(d)}
    z_peers = [{"fsdp": (z + k) % n} for k in range(1, n)]
    greet(z_peers + peers + [core_peer])
    used = [0]
    started = []

    def send(src, dst, peer, keep=True):
        index = used[0]
        used[0] += 1
        copy = pltpu.make_async_remote_copy(
            src_ref=src,
            dst_ref=dst,
            send_sem=send_sem.at[index],
            recv_sem=recv_sem.at[index],
            device_id=peer,
            device_id_type=MESH,
        )
        copy.start()
        if keep:
            started.append(copy)
        return copy

    flip_1 = place + 1 - 2 * (place % 2)
    flip_2 = place + 2 - 4 * (place // 2)
    across, corner, own, late = {}, {}, [], []

    def region(t, where, half=None):
        rows = ready[t].shape[0]
        start = (core * 4 + where) * rows
        if half is None:
            return wholes[t].at[rows_of(start, rows), :]
        return wholes[t].at[rows_of(start + half * (rows // 2), rows // 2), :]

    def spread_open(t):
        spot = region(t, place)
        across[t] = (send(ready[t], spot, peers[0]), send(ready[t], spot, peers[1]))
        late.append(send(ready[t], spot, core_peer))
        own.append(pltpu.make_async_copy(ready[t], spot, own_sem.at[t]))
        own[-1].start()

    def spread_turn(t):
        by_x, by_y = across[t]
        by_y.wait_recv()
        view = region(t, flip_2, 0)
        one = send(view, view, peers[0])
        view = region(t, flip_2)
        late.append(send(view, view, core_peer))
        by_x.wait_recv()
        view = region(t, flip_1, 1)
        corner[t] = (one, send(view, view, peers[1]))
        view = region(t, flip_1)
        late.append(send(view, view, core_peer))

    def spread_close(t):
        for copy in corner[t]:
            copy.wait_recv()
        view = region(t, 3 - place)
        late.append(send(view, view, core_peer))

    def finish(t):
        p = part[t]
        for k in range(1, n):
            third[t, k].wait_recv()

        @pl.loop(0, p // 16)
        def _(step):
            total = held[t][pl.ds(pl.multiple_of(place * p + step * 16, 16), 16), :].astype(jnp.float32)
            for k in range(1, n):
                at = pl.ds(pl.multiple_of((k - 1) * p + step * 16, 16), 16)
                total = total + from_z[t][at, :].astype(jnp.float32)
            outs[t][pl.ds(pl.multiple_of(step * 16, 16), 16), :] = total.astype(jnp.bfloat16)

    units = [(t, k) for t in range(count) for k in [*range(1, n), 0]]
    part = [rows // (8 * n) for rows, _ in plan]
    arrive, first, second, third = {}, {}, {}, {}

    def make(t, k, spare):
        half = 4 * part[t]
        tile = 128 * 1024 // half
        column = ((z + k) % n) * 2 * half
        offset = 0
        for (left, right), width in zip(pairs[t], plan[t][1]):
            tiles = width // tile

            @pl.loop(0, 2 * tiles)
            def _(step):
                own, index = step // tiles, step % tiles
                side = own * core + (1 - own) * (1 - core)
                source = pl.ds(pl.multiple_of(column + side * half, 128), half)
                row = own * (k * half) + (1 - own) * ((n + spare) * half)
                across = pl.ds(pl.multiple_of(index * tile, 128), tile)
                target = pl.ds(pl.multiple_of(offset + index * tile, 128), tile)
                block = left_product(left[:, source], right[:, across])
                held[t][rows_of(row, half), target] = block.astype(jnp.bfloat16)

            offset += width

    for i in range(len(units) + 6):
        if i < len(units):
            t, k = units[i]
            half, spare = 4 * part[t], i % 2
            if i >= 2 and units[i - 2][0] == t:
                arrive[i - 2].wait_send()
            make(t, k, spare)
            arrive[i] = send(
                held[t].at[pl.ds((n + spare) * half, half), :],
                from_core[t].at[pl.ds(k * half, half), :],
                core_peer,
                keep=i + 2 >= len(units) or units[i + 2][0] != t,
            )
        if small and i < 3:
            if i == 0:
                small_held[...] = small_ref[...]
            else:
                small_copy.wait()
                small_held[...] += small_got[i - 1]
            small_copy = send(small_held, small_got.at[i], [core_peer, *peers][i], keep=False)
        if small and i == 3:
            small_copy.wait()
            small_held[...] += small_got[2]
            width = small_out.shape[1]
            small_z_copies = [
                send(
                    small_held.at[:, pl.ds(pl.multiple_of(((z + k) % n) * width, 128), width)],
                    small_z.at[k - 1],
                    z_peers[k - 1],
                )
                for k in range(1, n)
            ]
        j = i - 1
        if 0 <= j < len(units):
            t, k = units[j]
            p, base = part[t], k * 4 * part[t]
            arrive[j].wait_recv()
            add_rows(held[t], base, from_core[t], base, 4 * p)
            if j % 2 == 0:
                first[j] = [
                    send(
                        held[t].at[rows_of(base + (2 * y + 1 - x_bit) * p, p), :],
                        from_first[t].at[pl.ds((2 * k + y) * p, p), :],
                        peers[0],
                    )
                    for y in range(2)
                ]
            else:
                first[j] = [
                    send(
                        held[t].at[rows_of(base + 2 * (1 - y_bit) * p, 2 * p), :],
                        from_first[t].at[pl.ds(2 * k * p, 2 * p), :],
                        peers[1],
                    )
                ]
        j = i - 3
        if 0 <= j < len(units):
            t, k = units[j]
            p, base = part[t], k * 4 * part[t]
            for copy in first[j]:
                copy.wait_recv()
            if j % 2 == 0:
                for y in range(2):
                    add_rows(held[t], base + (2 * y + x_bit) * p, from_first[t], (2 * k + y) * p, p)
                gone, peer = base + (2 * (1 - y_bit) + x_bit) * p, peers[1]
            else:
                add_rows(held[t], base + 2 * y_bit * p, from_first[t], 2 * k * p, 2 * p)
                gone, peer = base + (2 * y_bit + 1 - x_bit) * p, peers[0]
            second[j] = send(held[t].at[rows_of(gone, p), :], from_second[t].at[pl.ds(k * p, p), :], peer)
        j = i - 5
        if 0 <= j < len(units):
            t, k = units[j]
            p, base = part[t], k * 4 * part[t]
            second[j].wait_recv()
            add_rows(held[t], base + place * p, from_second[t], k * p, p)
            if k > 0:
                third[t, k] = send(
                    held[t].at[rows_of(base + place * p, p), :],
                    from_z[t].at[pl.ds((k - 1) * p, p), :],
                    z_peers[k - 1],
                )
        if small:
            for t in range(count - 1):
                if i == n * (t + 1) + 8:
                    finish(t)
                    spread_open(extra + t)
                if i == n * (t + 1) + 11:
                    spread_turn(extra + t)
            at = i - (len(units) - extra)
            if 0 <= at < extra:
                spread_open(at)
            if 0 <= at - 2 < extra:
                spread_turn(at - 2)
    if small:
        opened = {t for t in range(count - 1) if n * (t + 1) + 8 < len(units) + 6}
        for t in range(count):
            if t not in opened:
                finish(t)
                spread_open(extra + t)
        for t in range(extra + count):
            if t not in corner:
                spread_turn(t)
        for t in range(extra + count):
            spread_close(t)
        for copy in own:
            copy.wait()
        for copy in late:
            copy.wait_recv()
    else:
        for t in range(count):
            finish(t)

    if small:
        for copy in small_z_copies:
            copy.wait_recv()
        total = small_held[:, pl.ds(pl.multiple_of(z * width, 128), width)]
        for k in range(1, n):
            total = total + small_z[k - 1]
        small_out[...] = total
    for copy in started:
        copy.wait_send()


def sum_products(n, tensors, small, ready, collective_id):
    plan = [
        (pairs[0][0].shape[1], tuple(right.shape[1] for _, right in pairs)) for pairs in tensors
    ]
    count = len(plan)
    operands = [side for pairs in tensors for pair in pairs for side in pair]
    shapes = [(rows, sum(widths)) for rows, widths in plan]
    out_shape = [jax.ShapeDtypeStruct((r // (8 * n), c), jnp.bfloat16) for r, c in shapes]

    def room(over, under):
        return [pltpu.VMEM((r * over // under, c), jnp.bfloat16) for r, c in shapes]

    scratch = [
        *room(n + 2, 2 * n),
        *room(1, 2),
        *room(1, 4),
        *room(1, 8),
        *room(n - 1, 8 * n),
    ]
    copies = count * (5 * n - 1)
    whole = pl.BlockSpec(memory_space=pltpu.VMEM)
    out_specs = [whole] * count
    if small is not None:
        operands += [small, *ready]
        depth, width = small.shape
        pieces = [pltpu.VMEM(s.shape, jnp.bfloat16) for s in out_shape]
        out_shape = [
            *[jax.ShapeDtypeStruct((8 * s.shape[0], s.shape[1]), s.dtype) for s in [*ready, *out_shape]],
            jax.ShapeDtypeStruct((depth, width // n), jnp.float32),
        ]
        out_specs = [pl.BlockSpec(memory_space=pltpu.HBM)] * (len(out_shape) - 1) + [whole]
        scratch = pieces + scratch + [
            pltpu.VMEM((depth, width), jnp.float32),
            pltpu.VMEM((3, depth, width), jnp.float32),
            pltpu.VMEM((n - 1, depth, width // n), jnp.float32),
            pltpu.SemaphoreType.DMA((len(ready) + count,)),
        ]
        copies += 3 + n - 1 + 8 * (len(ready) + count)
    return pl.pallas_call(
        partial(sums_kernel, n, plan, 0 if small is None else len(ready)),
        out_shape=out_shape,
        in_specs=[whole] * len(operands),
        out_specs=out_specs,
        scratch_shapes=[
            *scratch,
            pltpu.SemaphoreType.DMA((copies,)),
            pltpu.SemaphoreType.DMA((copies,)),
        ],
        compiler_params=pltpu.CompilerParams(
            collective_id=collective_id, has_side_effects=True, vmem_limit_bytes=63 * 1024 * 1024
        ),
        name="sum_products",
    )(*operands)


EARLY = (6, 7, 4, 5)
LATE = (2, 0, 1, 3)


def fallback_reduce(pairs):
    grad = jnp.concatenate([left_product(left, right) for left, right in pairs], axis=1)
    part = lax.psum_scatter(grad.astype(jnp.bfloat16), "fsdp", scatter_dimension=0, tiled=True)
    return lax.psum(part, "dp")


def on_device(
    fast,
    n,
    inputs,
    cotangent,
    lengths,
    buckets,
    ffn1_in,
    ffn1_out,
    attn_in,
    attn_out,
    conv_in,
    conv_out,
    ffn2_in,
    ffn2_out,
    norm_gains,
    pos_bias,
    kernel,
):
    shards = [ffn1_in, ffn1_out, attn_in, attn_out, conv_in, conv_out, ffn2_in, ffn2_out]
    width = norm_gains.shape[1]
    vectors = jnp.concatenate(
        [norm_gains, pos_bias, kernel, jnp.zeros((3, width), norm_gains.dtype)], axis=0
    )
    if fast:
        gathered = gather_all(n, shards, vectors, 0)
        weights, vec = gathered[:8], gathered[8]
        vec = vec.reshape(n, 16, width).transpose(1, 0, 2).reshape(16, D)
    else:
        weights = [lax.all_gather(s, "fsdp", axis=0, tiled=True) for s in shards]
        vec = lax.all_gather(vectors, "fsdp", axis=1, tiled=True)
    vec = vec.astype(jnp.float32)
    gains, biases, taps = vec[0:6], vec[6:8], vec[8:13]
    plans = [frame_plan(lengths[m], buckets[m]) for m in range(MICRO)]
    allowed = jnp.stack([p[0] for p in plans], axis=0).astype(jnp.float32)
    tap_masks = jnp.concatenate([p[1] for p in plans], axis=1)
    table_low = sinusoid(1).astype(jnp.bfloat16)
    mirror_low = sinusoid(-1).astype(jnp.bfloat16)

    stream = inputs.astype(jnp.float32)
    branch, kept_one = ffn_forward(stream, gains[0], weights[0], weights[1])
    section_one = stream + 0.5 * branch
    positions = matmul(table_low, weights[2][:, 3 * D :]).astype(jnp.bfloat16)
    mirrored = matmul(mirror_low, weights[2][:, 3 * D :]).astype(jnp.bfloat16)
    weight_qkv = weights[2][:, : 3 * D]
    branch, kept_two = attn_forward(
        section_one, gains[1], weight_qkv, weights[3], biases, positions, allowed
    )
    section_two = section_one + branch
    branch, kept_three = conv_forward(
        section_two, gains[2], gains[3], weights[4], weights[5], taps, tap_masks
    )
    section_three = section_two + branch
    branch, kept_four = ffn_forward(section_three, gains[4], weights[6], weights[7])
    section_four = section_three + 0.5 * branch
    final_out, final_pull = jax.vjp(layer_norm, section_four, gains[5])
    grad_stream, grad_final = final_pull(cotangent.astype(jnp.float32))

    grad_values, grad_vec4, grad_in4, grad_out4 = ffn_backward(
        0.5 * grad_stream, kept_four, weights[6], weights[7]
    )
    sums = [None] * 8
    grad_stream = grad_stream + grad_values
    grad_values, grad_vec3, grad_in3, grad_out3 = conv_backward(
        grad_stream, kept_three, weights[4], weights[5]
    )
    grad_stream = grad_stream + grad_values
    grad_values, grad_vec2, grad_in2, grad_out2, grad_pos = attn_backward(
        grad_stream, kept_two, weight_qkv, weights[3], biases, mirrored
    )
    grad_stream = grad_stream + grad_values
    grad_values, grad_vec1, grad_in1, grad_out1 = ffn_backward(
        0.5 * grad_stream, kept_one, weights[0], weights[1]
    )
    grad_in2 = grad_in2 + [(mirror_low, grad_pos)]
    grad_stream = grad_stream + grad_values

    grad_vectors = jnp.concatenate(
        [
            grad_vec1,
            grad_vec2[0:1],
            grad_vec3[0:2],
            grad_vec4,
            grad_final[None],
            grad_vec2[1:3],
            grad_vec3[2:7],
            jnp.zeros((3, D), jnp.float32),
        ],
        axis=0,
    )
    tensors = [grad_in1, grad_out1, grad_in2, grad_out2, grad_in3, grad_out3, grad_in4, grad_out4]
    if fast:
        early = sum_products(n, [tensors[i] for i in EARLY], None, (), 1)
        *wholes, grad_small = sum_products(n, [tensors[i] for i in LATE], grad_vectors, early, 2)
        for index, total in zip(EARLY + LATE, wholes):
            sums[index] = total
    else:
        sums = [fallback_reduce(pairs) for pairs in tensors]
        grad_small = lax.psum(
            lax.psum_scatter(grad_vectors, "fsdp", scatter_dimension=1, tiled=True), "dp"
        )
    grads = [s.astype(jnp.float32) for s in sums]
    return (
        final_out.astype(jnp.bfloat16),
        grad_stream,
        *grads,
        grad_small[0:6],
        grad_small[6:8],
        grad_small[8:13],
    )


def solution(mesh):
    in_specs = (
        P(("dp", "fsdp"), None),
        P(("dp", "fsdp"), None),
        P(("dp", "fsdp"), None),
        P(("dp", "fsdp")),
        P("fsdp", None),
        P("fsdp", None),
        P("fsdp", None),
        P("fsdp", None),
        P("fsdp", None),
        P("fsdp", None),
        P("fsdp", None),
        P("fsdp", None),
        P(None, "fsdp"),
        P(None, "fsdp"),
        P(None, "fsdp"),
    )
    out_specs = (
        P(("dp", "fsdp"), None),
        P(("dp", "fsdp"), None),
        P("fsdp", None),
        P("fsdp", None),
        P("fsdp", None),
        P("fsdp", None),
        P("fsdp", None),
        P("fsdp", None),
        P("fsdp", None),
        P("fsdp", None),
        P(None, "fsdp"),
        P(None, "fsdp"),
        P(None, "fsdp"),
    )
    sizes = dict(mesh.shape)
    n = sizes["fsdp"]
    fast = sizes["dp"] == 8 and n == 4
    return jax.shard_map(
        partial(on_device, fast, n), mesh=mesh, in_specs=in_specs, out_specs=out_specs, check_vma=False
    )
```

```python
from functools import partial
import math

import jax
import jax.numpy as jnp
from jax import lax
from jax.experimental import pallas as pl
from jax.experimental.pallas import tpu as pltpu
from jax.sharding import PartitionSpec as P

MESH = pl.DeviceIdType.MESH

D = 1024
HEADS = 8
HEAD_DIM = 128
KERNEL = 5
BUCKET = 64
MICRO = 2
FRAMES = 192
SLOTS = 3


def matmul(left_side, right_side):
    return jnp.dot(left_side, right_side, preferred_element_type=jnp.float32)


def left_product(left_side, right_side):
    return lax.dot_general(
        left_side, right_side, (((0,), (0,)), ((), ())), preferred_element_type=jnp.float32
    )


def right_product(left_side, right_side):
    return lax.dot_general(
        left_side, right_side, (((1,), (1,)), ((), ())), preferred_element_type=jnp.float32
    )


def layer_norm(values, gain_row):
    centred = values - jnp.mean(values, axis=-1, keepdims=True)
    spread = jnp.mean(centred * centred, axis=-1, keepdims=True)
    return centred * lax.rsqrt(spread + 1e-05) * gain_row


def swish_act(values):
    return values * jax.nn.sigmoid(values)


def neighbour(values, offset):
    if offset > 0:
        filler = jnp.zeros((offset,) + values.shape[1:], values.dtype)
        return jnp.concatenate([values[offset:], filler], axis=0)
    if offset < 0:
        filler = jnp.zeros((-offset,) + values.shape[1:], values.dtype)
        return jnp.concatenate([filler, values[:offset]], axis=0)
    return values


def frame_plan(utter_len, bucket_id):
    position = jnp.arange(FRAMES, dtype=jnp.int32)
    bucket_len = BUCKET * (bucket_id + 1)
    segment = position // bucket_len
    offset_in = position - segment * bucket_len
    slot_index = jnp.arange(SLOTS, dtype=jnp.int32)
    slot_limit = jnp.sum(
        jnp.where(segment[:, None] == slot_index[None, :], utter_len[None, :], 0), axis=1
    )
    is_valid = offset_in < slot_limit
    allowed = (segment[:, None] == segment[None, :]) & is_valid[None, :] | (
        position[:, None] == position[None, :]
    )
    tap_list = []
    for tap_index in range(KERNEL):
        shift_by = tap_index - KERNEL // 2
        same_slot = (neighbour(segment + 1, shift_by) == segment + 1) & neighbour(
            is_valid, shift_by
        )
        tap_list.append(same_slot.astype(jnp.float32))
    return (allowed, jnp.stack(tap_list, axis=0))


def sinusoid(sign):
    column = jnp.arange(D, dtype=jnp.int32)
    rates = jnp.exp((column // 2).astype(jnp.float32) * (-2.0 * math.log(10000.0) / D))
    phase = (column % 2).astype(jnp.float32) * (0.5 * math.pi)
    coarse = sign * (16 * jnp.arange(2 * FRAMES // 16, dtype=jnp.int32) - (FRAMES - 1)).astype(jnp.float32)
    fine = sign * jnp.arange(16, dtype=jnp.int32).astype(jnp.float32)
    angle = coarse[:, None] * rates[None, :]
    rest = fine[:, None] * rates[None, :] + phase[None, :]
    sin_a, cos_a = lax.optimization_barrier((jnp.sin(angle), jnp.cos(angle)))
    sin_b, cos_b = lax.optimization_barrier((jnp.sin(rest), jnp.cos(rest)))
    table = sin_a[:, None] * cos_b[None] + cos_a[:, None] * sin_b[None]
    return table.reshape(2 * FRAMES, D)


def depthwise(values, kernel_rows, tap_masks):
    running = jnp.zeros_like(values)
    for tap_index in range(KERNEL):
        moved = neighbour(values, tap_index - KERNEL // 2)
        running = running + moved * tap_masks[tap_index][:, None] * kernel_rows[tap_index][None, :]
    return running


def conv_inner(gated, gain_inner, kernel_rows, tap_masks):
    gated_out = gated[:, :D] * jax.nn.sigmoid(gated[:, D:])
    return swish_act(layer_norm(depthwise(gated_out, kernel_rows, tap_masks), gain_inner))


def ffn_forward(values, gain_row, weight_in, weight_out):
    normed, norm_pull = jax.vjp(layer_norm, values, gain_row)
    normed_low = normed.astype(jnp.bfloat16)
    hidden = matmul(normed_low, weight_in)
    active = swish_act(hidden).astype(jnp.bfloat16)
    return (matmul(active, weight_out), (norm_pull, normed_low, hidden, active))


def ffn_backward(grad_branch, kept_state, weight_in, weight_out):
    norm_pull, normed_low, hidden, active = kept_state
    grad_out = grad_branch.astype(jnp.bfloat16)
    grad_active = right_product(grad_out, weight_out)
    swish_value, swish_pull = jax.vjp(swish_act, hidden)
    grad_hidden = swish_pull(grad_active)[0].astype(jnp.bfloat16)
    grad_normed = right_product(grad_hidden, weight_in)
    grad_values, grad_gain = norm_pull(grad_normed)
    return (grad_values, grad_gain[None], [(normed_low, grad_hidden)], [(active, grad_out)])


TABLE = 2 * FRAMES
SCALE = HEAD_DIM ** (-0.5)


def nn(left_side, right_side):
    return lax.dot_general(
        left_side, right_side, (((1,), (0,)), ((), ())), preferred_element_type=jnp.float32
    )


def attend_kernel(q_ref, k_ref, v_ref, bias_ref, pos_ref, allow_ref, mixed_ref, prob_ref):
    query = q_ref[...].astype(jnp.float32)
    query_u = ((query + bias_ref[0:1, :]) * SCALE).astype(jnp.bfloat16)
    query_v = ((query + bias_ref[1:2, :]) * SCALE).astype(jnp.bfloat16)
    table = right_product(query_v, pos_ref[...])
    for m in range(MICRO):
        rows = slice(m * FRAMES, (m + 1) * FRAMES)
        content = right_product(query_u[rows], k_ref[rows, :])
        moved = pltpu.roll(table[rows], TABLE - FRAMES + 1, 1, stride=1, stride_axis=0)
        scores = jnp.where(allow_ref[m] > 0, content + moved[:, :FRAMES], -1e30)
        weight = jnp.exp(scores - jnp.max(scores, axis=-1, keepdims=True))
        prob = (weight / jnp.sum(weight, axis=-1, keepdims=True)).astype(jnp.bfloat16)
        prob_ref[m, 0] = prob
        mixed_ref[rows, :] = nn(prob, v_ref[rows, :]).astype(jnp.bfloat16)


def attend_back_kernel(
    q_ref, k_ref, v_ref, bias_ref, pos_ref, prob_ref, grad_ref, dq_ref, dk_ref, dv_ref, dpos_ref, dbias_ref
):
    query = q_ref[...].astype(jnp.float32)
    query_u = ((query + bias_ref[0:1, :]) * SCALE).astype(jnp.bfloat16)
    query_v = ((query + bias_ref[1:2, :]) * SCALE).astype(jnp.bfloat16)
    across = lax.broadcasted_iota(jnp.int32, (FRAMES, FRAMES), 0)
    down = lax.broadcasted_iota(jnp.int32, (FRAMES, FRAMES), 1)
    swap = jnp.where(across + down == FRAMES - 1, 1.0, 0.0).astype(jnp.bfloat16)
    tables, grads_u = [], []
    for m in range(MICRO):
        rows = slice(m * FRAMES, (m + 1) * FRAMES)
        prob = prob_ref[m, 0]
        grad = grad_ref[rows, :]
        dv_ref[rows, :] = left_product(prob, grad).astype(jnp.bfloat16)
        grad_prob = right_product(grad, v_ref[rows, :])
        wide = prob.astype(jnp.float32)
        inner = jnp.sum(wide * grad_prob, axis=-1, keepdims=True)
        grad_score = wide * (grad_prob - inner)
        low = grad_score.astype(jnp.bfloat16)
        grads_u.append(nn(low, k_ref[rows, :]))
        dk_ref[rows, :] = left_product(low, query_u[rows]).astype(jnp.bfloat16)
        turned = nn(low, swap)
        padded = jnp.concatenate([turned, jnp.zeros_like(turned)], axis=1)
        tables.append(pltpu.roll(padded, 0, 1, stride=1, stride_axis=0))
    table = jnp.concatenate(tables, axis=0).astype(jnp.bfloat16)
    grad_u = jnp.concatenate(grads_u, axis=0) * SCALE
    grad_v = nn(table, pos_ref[...]) * SCALE
    dpos_ref[...] = left_product(table, query_v).astype(jnp.bfloat16)
    dq_ref[...] = (grad_u + grad_v).astype(jnp.bfloat16)
    dbias_ref[0:1, :] = jnp.sum(grad_u, axis=0, keepdims=True)
    dbias_ref[1:2, :] = jnp.sum(grad_v, axis=0, keepdims=True)


def head_spec(rows, offset=0):
    return pl.BlockSpec((rows, HEAD_DIM), lambda h: (0, offset + h))


PROB_SPEC = pl.BlockSpec((MICRO, 1, FRAMES, FRAMES), lambda h: (0, h, 0, 0))


def attend(project, bias, positions, allowed):
    rows = project.shape[0]
    return pl.pallas_call(
        attend_kernel,
        grid=(HEADS,),
        out_shape=[
            jax.ShapeDtypeStruct((rows, D), jnp.bfloat16),
            jax.ShapeDtypeStruct((MICRO, HEADS, FRAMES, FRAMES), jnp.bfloat16),
        ],
        in_specs=[
            head_spec(rows),
            head_spec(rows, HEADS),
            head_spec(rows, 2 * HEADS),
            head_spec(2),
            head_spec(TABLE),
            pl.BlockSpec((MICRO, FRAMES, FRAMES), lambda h: (0, 0, 0)),
        ],
        out_specs=[head_spec(rows), PROB_SPEC],
        name="attend",
    )(project, project, project, bias, positions, allowed)


def attend_back(project, bias, positions, prob, grad_mixed):
    rows = project.shape[0]
    wide = jax.ShapeDtypeStruct((rows, D), jnp.bfloat16)
    return pl.pallas_call(
        attend_back_kernel,
        grid=(HEADS,),
        out_shape=[
            wide,
            wide,
            wide,
            jax.ShapeDtypeStruct((TABLE, D), jnp.bfloat16),
            jax.ShapeDtypeStruct((2, D), jnp.float32),
        ],
        in_specs=[
            head_spec(rows),
            head_spec(rows, HEADS),
            head_spec(rows, 2 * HEADS),
            head_spec(2),
            head_spec(TABLE),
            PROB_SPEC,
            head_spec(rows),
        ],
        out_specs=[head_spec(rows), head_spec(rows), head_spec(rows), head_spec(TABLE), head_spec(2)],
        name="attend_back",
    )(project, project, project, bias, positions, prob, grad_mixed)


def attn_forward(values, gain_row, weight_qkv, weight_out, bias, positions, allowed):
    normed, norm_pull = jax.vjp(layer_norm, values, gain_row)
    normed_low = normed.astype(jnp.bfloat16)
    project = matmul(normed_low, weight_qkv).astype(jnp.bfloat16)
    mixed_heads, prob = attend(project, bias, positions, allowed)
    kept_state = (norm_pull, normed_low, project, prob, mixed_heads)
    return (matmul(mixed_heads, weight_out), kept_state)


def attn_backward(grad_res, kept_state, weight_qkv, weight_out, bias, positions):
    norm_pull, normed_low, project, prob, mixed_heads = kept_state
    grad_branch = grad_res.astype(jnp.bfloat16)
    grad_mixed = right_product(grad_branch, weight_out).astype(jnp.bfloat16)
    grad_q, grad_k, grad_v, grad_pos, grad_bias = attend_back(
        project, bias, positions, prob, grad_mixed
    )
    grad_project = jnp.concatenate([grad_q, grad_k, grad_v], axis=1)
    grad_normed = right_product(grad_project, weight_qkv)
    grad_values, grad_gain = norm_pull(grad_normed)
    grad_vec = jnp.concatenate([grad_gain[None], grad_bias], axis=0)
    return (grad_values, grad_vec, [(normed_low, grad_project)], [(mixed_heads, grad_branch)], grad_pos)


def conv_forward(values, gain_row, gain_inner, weight_in, weight_out, kernel_rows, tap_masks):
    normed, norm_pull = jax.vjp(layer_norm, values, gain_row)
    normed_low = normed.astype(jnp.bfloat16)
    gated = matmul(normed_low, weight_in)
    active, inner_pull = jax.vjp(
        partial(conv_inner, tap_masks=tap_masks), gated, gain_inner, kernel_rows
    )
    active_low = active.astype(jnp.bfloat16)
    return (matmul(active_low, weight_out), (norm_pull, normed_low, inner_pull, active_low))


def conv_backward(grad_res, kept_state, weight_in, weight_out):
    norm_pull, normed_low, inner_pull, active_low = kept_state
    grad_branch = grad_res.astype(jnp.bfloat16)
    grad_active = right_product(grad_branch, weight_out)
    grad_gated, grad_inner, grad_taps = inner_pull(grad_active)
    grad_gated_low = grad_gated.astype(jnp.bfloat16)
    grad_normed = right_product(grad_gated_low, weight_in)
    grad_values, grad_gain = norm_pull(grad_normed)
    grad_vec = jnp.concatenate([grad_gain[None], grad_inner[None], grad_taps], axis=0)
    return (grad_values, grad_vec, [(normed_low, grad_gated_low)], [(active_low, grad_branch)])


def other_core(d):
    return d + 1 - 2 * (d % 2)


def flip_x(d):
    return d + 2 - 4 * ((d // 2) % 2)


def flip_y(d):
    return d + 4 - 8 * ((d // 4) % 2)


def greet(peers):
    barrier = pltpu.get_barrier_semaphore()
    for peer in peers:
        pl.semaphore_signal(barrier, inc=1, device_id=peer, device_id_type=MESH)
    pl.semaphore_wait(barrier, len(peers))


def rows_of(start, count):
    return pl.ds(pl.multiple_of(start, 16), count)


ORDER = (4, 0, 1, 2, 6, 7, 3, 5)
DIRECT = (3, 5)


def gather_kernel(n, count, *refs):
    shards = refs[: count + 1]
    fulls = refs[count + 1 : 2 * count + 2]
    send_sem, recv_sem = refs[2 * count + 2 :]
    z = lax.axis_index("fsdp")
    d = lax.axis_index("dp")
    core, place = d % 2, d // 2
    x_peer, y_peer, core_peer = {"dp": flip_x(d)}, {"dp": flip_y(d)}, {"dp": other_core(d)}
    up, down = {"fsdp": (z + 1) % n}, {"fsdp": (z + n - 1) % n}
    greet([up, down, x_peer, y_peer, core_peer])
    used = [0]
    started = []

    def send(src, dst, peer):
        index = used[0]
        used[0] += 1
        copy = pltpu.make_async_remote_copy(
            src_ref=src,
            dst_ref=dst,
            send_sem=send_sem.at[index],
            recv_sem=recv_sem.at[index],
            device_id=peer,
            device_id_type=MESH,
        )
        copy.start()
        started.append(copy)
        return copy

    flip_1 = place + 1 - 2 * (place % 2)
    flip_2 = place + 2 - 4 * (place // 2)

    def span(t, owner):
        depth = shards[t].shape[0]
        if t == count:
            return rows_of(owner * depth, depth)
        if t in DIRECT:
            return rows_of(owner * depth + core * (depth // 2), depth // 2)
        return rows_of(owner * depth + (core * 4 + place) * (depth // 8), depth // 8)

    first = {}

    def launch(t):
        view = shards[t].at[span(t, 0), :]
        first[t, 1] = send(view, fulls[t].at[span(t, z), :], up)
        first[t, 3] = send(view, fulls[t].at[span(t, z), :], down)

    def relay(t):
        view = fulls[t].at[span(t, (z + n - 1) % n), :]
        first[t, 2] = send(view, view, up)

    def piece(t, k, where, half=None):
        depth = shards[t].shape[0]
        part = depth // 8
        start = ((z + n - k) % n) * depth + (core * 4 + where) * part
        if half is None:
            return fulls[t].at[rows_of(start, part), :]
        return fulls[t].at[rows_of(start + half * (part // 2), part // 2), :]

    late = []

    def to_core(t, k):
        depth = shards[t].shape[0]
        half = depth // 2
        view = fulls[t].at[rows_of(((z + n - k) % n) * depth + core * half, half), :]
        late.append(send(view, view, core_peer))

    launch(ORDER[0])
    launch(count)
    launch(ORDER[1])
    for t in [*ORDER, count]:
        depth = shards[t].shape[0]
        late.append(send(shards[t], fulls[t].at[rows_of(z * depth, depth), :], core_peer))
    stages = [(t, k) for t in ORDER if t not in DIRECT for k in (1, 3, 2)]
    across, corner = {}, {}
    for i in range(len(stages) + 2):
        if i < len(stages):
            t, k = stages[i]
            first[t, k].wait_recv()
            if k == 1:
                relay(t)
                following = ORDER.index(t) + 2
                if following < count:
                    launch(ORDER[following])
            mine = piece(t, k, place)
            across[i] = (send(mine, mine, x_peer), send(mine, mine, y_peer))
        if 0 <= i - 1 < len(stages):
            t, k = stages[i - 1]
            by_x, by_y = across[i - 1]
            by_y.wait_recv()
            view = piece(t, k, flip_2, 0)
            one = send(view, view, x_peer)
            by_x.wait_recv()
            view = piece(t, k, flip_1, 1)
            corner[i - 1] = (one, send(view, view, y_peer))
        if 0 <= i - 2 < len(stages):
            for copy in corner[i - 2]:
                copy.wait_recv()
            to_core(*stages[i - 2])
    for t in [*DIRECT, count]:
        first[t, 1].wait_recv()
        relay(t)
    for k in (1, 3, 2):
        for t in DIRECT:
            if k > 1:
                first[t, k].wait_recv()
            to_core(t, k)
    for k in (2, 3):
        first[count, k].wait_recv()
    for copy in late:
        copy.wait_recv()
    for copy in started:
        copy.wait_send()


def gather_all(n, shards, small, collective_id):
    count = len(shards)
    given = list(shards) + [small]
    copies = count * (n - 1) * 6 + n + count
    return pl.pallas_call(
        partial(gather_kernel, n, count),
        out_shape=[jax.ShapeDtypeStruct((n * s.shape[0], s.shape[1]), s.dtype) for s in given],
        in_specs=[pl.BlockSpec(memory_space=pltpu.HBM)] * (count + 1),
        out_specs=[pl.BlockSpec(memory_space=pltpu.HBM)] * (count + 1),
        scratch_shapes=[pltpu.SemaphoreType.DMA((copies,)), pltpu.SemaphoreType.DMA((copies,))],
        compiler_params=pltpu.CompilerParams(collective_id=collective_id, has_side_effects=True),
        name="gather_weights",
    )(*given)


def add_rows(dst, dst_row, src, src_row, count):
    @pl.loop(0, count // 16)
    def _(step):
        at = pl.ds(pl.multiple_of(dst_row + step * 16, 16), 16)
        take = pl.ds(pl.multiple_of(src_row + step * 16, 16), 16)
        total = dst[at, :].astype(jnp.float32) + src[take, :].astype(jnp.float32)
        dst[at, :] = total.astype(jnp.bfloat16)


def sums_kernel(n, plan, extra, *refs):
    small = extra > 0
    count = len(plan)
    inputs = sum(2 * len(widths) for _, widths in plan)
    operands = list(refs[:inputs])
    refs = refs[inputs:]
    if small:
        small_ref, refs = refs[0], refs[1:]
        ready, refs = list(refs[:extra]), refs[extra:]
        wholes, refs = refs[: extra + count], refs[extra + count :]
        small_out, refs = refs[0], refs[1:]
        outs, refs = refs[:count], refs[count:]
    else:
        outs, refs = refs[:count], refs[count:]
    held, refs = refs[:count], refs[count:]
    from_core, refs = refs[:count], refs[count:]
    from_first, refs = refs[:count], refs[count:]
    from_second, refs = refs[:count], refs[count:]
    from_z, refs = refs[:count], refs[count:]
    if small:
        (small_held, small_got, small_z, own_sem), refs = refs[:4], refs[4:]
        ready += list(outs)
    send_sem, recv_sem = refs
    pairs = []
    for _, widths in plan:
        pairs.append([(operands.pop(0), operands.pop(0)) for _ in widths])
    z = lax.axis_index("fsdp")
    d = lax.axis_index("dp")
    core, place = d % 2, d // 2
    x_bit, y_bit = place % 2, place // 2
    peers = [{"dp": flip_x(d)}, {"dp": flip_y(d)}]
    core_peer = {"dp": other_core(d)}
    z_peers = [{"fsdp": (z + k) % n} for k in range(1, n)]
    greet(z_peers + peers + [core_peer])
    used = [0]
    started = []

    def send(src, dst, peer, keep=True):
        index = used[0]
        used[0] += 1
        copy = pltpu.make_async_remote_copy(
            src_ref=src,
            dst_ref=dst,
            send_sem=send_sem.at[index],
            recv_sem=recv_sem.at[index],
            device_id=peer,
            device_id_type=MESH,
        )
        copy.start()
        if keep:
            started.append(copy)
        return copy

    flip_1 = place + 1 - 2 * (place % 2)
    flip_2 = place + 2 - 4 * (place // 2)
    across, corner, own, late = {}, {}, [], []

    def region(t, where, half=None):
        rows = ready[t].shape[0]
        start = (core * 4 + where) * rows
        if half is None:
            return wholes[t].at[rows_of(start, rows), :]
        return wholes[t].at[rows_of(start + half * (rows // 2), rows // 2), :]

    def spread_open(t):
        spot = region(t, place)
        across[t] = (send(ready[t], spot, peers[0]), send(ready[t], spot, peers[1]))
        late.append(send(ready[t], spot, core_peer))
        own.append(pltpu.make_async_copy(ready[t], spot, own_sem.at[t]))
        own[-1].start()

    def spread_turn(t):
        by_x, by_y = across[t]
        by_y.wait_recv()
        view = region(t, flip_2, 0)
        one = send(view, view, peers[0])
        view = region(t, flip_2)
        late.append(send(view, view, core_peer))
        by_x.wait_recv()
        view = region(t, flip_1, 1)
        corner[t] = (one, send(view, view, peers[1]))
        view = region(t, flip_1)
        late.append(send(view, view, core_peer))

    def spread_close(t):
        for copy in corner[t]:
            copy.wait_recv()
        view = region(t, 3 - place)
        late.append(send(view, view, core_peer))

    def finish(t):
        p = part[t]
        for k in range(1, n):
            third[t, k].wait_recv()

        @pl.loop(0, p // 16)
        def _(step):
            total = held[t][pl.ds(pl.multiple_of(place * p + step * 16, 16), 16), :].astype(jnp.float32)
            for k in range(1, n):
                at = pl.ds(pl.multiple_of((k - 1) * p + step * 16, 16), 16)
                total = total + from_z[t][at, :].astype(jnp.float32)
            outs[t][pl.ds(pl.multiple_of(step * 16, 16), 16), :] = total.astype(jnp.bfloat16)

    units = [(t, k) for t in range(count) for k in [*range(1, n), 0]]
    part = [rows // (8 * n) for rows, _ in plan]
    arrive, first, second, third = {}, {}, {}, {}

    def make(t, k, spare):
        half = 4 * part[t]
        tile = 128 * 1024 // half
        column = ((z + k) % n) * 2 * half
        offset = 0
        for (left, right), width in zip(pairs[t], plan[t][1]):
            tiles = width // tile

            @pl.loop(0, 2 * tiles)
            def _(step):
                own, index = step // tiles, step % tiles
                side = own * core + (1 - own) * (1 - core)
                source = pl.ds(pl.multiple_of(column + side * half, 128), half)
                row = own * (k * half) + (1 - own) * ((n + spare) * half)
                across = pl.ds(pl.multiple_of(index * tile, 128), tile)
                target = pl.ds(pl.multiple_of(offset + index * tile, 128), tile)
                block = left_product(left[:, source], right[:, across])
                held[t][rows_of(row, half), target] = block.astype(jnp.bfloat16)

            offset += width

    for i in range(len(units) + 6):
        if i < len(units):
            t, k = units[i]
            half, spare = 4 * part[t], i % 2
            if i >= 2 and units[i - 2][0] == t:
                arrive[i - 2].wait_send()
            make(t, k, spare)
            arrive[i] = send(
                held[t].at[pl.ds((n + spare) * half, half), :],
                from_core[t].at[pl.ds(k * half, half), :],
                core_peer,
                keep=i + 2 >= len(units) or units[i + 2][0] != t,
            )
        if small and i < 3:
            if i == 0:
                small_held[...] = small_ref[...]
            else:
                small_copy.wait()
                small_held[...] += small_got[i - 1]
            small_copy = send(small_held, small_got.at[i], [core_peer, *peers][i], keep=False)
        if small and i == 3:
            small_copy.wait()
            small_held[...] += small_got[2]
            width = small_out.shape[1]
            small_z_copies = [
                send(
                    small_held.at[:, pl.ds(pl.multiple_of(((z + k) % n) * width, 128), width)],
                    small_z.at[k - 1],
                    z_peers[k - 1],
                )
                for k in range(1, n)
            ]
        j = i - 1
        if 0 <= j < len(units):
            t, k = units[j]
            p, base = part[t], k * 4 * part[t]
            arrive[j].wait_recv()
            add_rows(held[t], base, from_core[t], base, 4 * p)
            if j % 2 == 0:
                first[j] = [
                    send(
                        held[t].at[rows_of(base + (2 * y + 1 - x_bit) * p, p), :],
                        from_first[t].at[pl.ds((2 * k + y) * p, p), :],
                        peers[0],
                    )
                    for y in range(2)
                ]
            else:
                first[j] = [
                    send(
                        held[t].at[rows_of(base + 2 * (1 - y_bit) * p, 2 * p), :],
                        from_first[t].at[pl.ds(2 * k * p, 2 * p), :],
                        peers[1],
                    )
                ]
        j = i - 3
        if 0 <= j < len(units):
            t, k = units[j]
            p, base = part[t], k * 4 * part[t]
            for copy in first[j]:
                copy.wait_recv()
            if j % 2 == 0:
                for y in range(2):
                    add_rows(held[t], base + (2 * y + x_bit) * p, from_first[t], (2 * k + y) * p, p)
                gone, peer = base + (2 * (1 - y_bit) + x_bit) * p, peers[1]
            else:
                add_rows(held[t], base + 2 * y_bit * p, from_first[t], 2 * k * p, 2 * p)
                gone, peer = base + (2 * y_bit + 1 - x_bit) * p, peers[0]
            second[j] = send(held[t].at[rows_of(gone, p), :], from_second[t].at[pl.ds(k * p, p), :], peer)
        j = i - 5
        if 0 <= j < len(units):
            t, k = units[j]
            p, base = part[t], k * 4 * part[t]
            second[j].wait_recv()
            add_rows(held[t], base + place * p, from_second[t], k * p, p)
            if k > 0:
                third[t, k] = send(
                    held[t].at[rows_of(base + place * p, p), :],
                    from_z[t].at[pl.ds((k - 1) * p, p), :],
                    z_peers[k - 1],
                )
        if small:
            for t in range(count - 1):
                if i == n * (t + 1) + 8:
                    finish(t)
                    spread_open(extra + t)
                if i == n * (t + 1) + 11:
                    spread_turn(extra + t)
            at = i - 1
            if 0 <= at < extra:
                spread_open(at)
            if 0 <= at - 2 < extra:
                spread_turn(at - 2)
    if small:
        opened = {t for t in range(count - 1) if n * (t + 1) + 8 < len(units) + 6}
        for t in range(count):
            if t not in opened:
                finish(t)
                spread_open(extra + t)
        for t in range(extra + count):
            if t not in corner:
                spread_turn(t)
        for t in range(extra + count):
            spread_close(t)
        for copy in own:
            copy.wait()
        for copy in late:
            copy.wait_recv()
    else:
        for t in range(count):
            finish(t)

    if small:
        for copy in small_z_copies:
            copy.wait_recv()
        total = small_held[:, pl.ds(pl.multiple_of(z * width, 128), width)]
        for k in range(1, n):
            total = total + small_z[k - 1]
        small_out[...] = total
    for copy in started:
        copy.wait_send()


def sum_products(n, tensors, small, ready, collective_id):
    plan = [
        (pairs[0][0].shape[1], tuple(right.shape[1] for _, right in pairs)) for pairs in tensors
    ]
    count = len(plan)
    operands = [side for pairs in tensors for pair in pairs for side in pair]
    shapes = [(rows, sum(widths)) for rows, widths in plan]
    out_shape = [jax.ShapeDtypeStruct((r // (8 * n), c), jnp.bfloat16) for r, c in shapes]

    def room(over, under):
        return [pltpu.VMEM((r * over // under, c), jnp.bfloat16) for r, c in shapes]

    scratch = [
        *room(n + 2, 2 * n),
        *room(1, 2),
        *room(1, 4),
        *room(1, 8),
        *room(n - 1, 8 * n),
    ]
    copies = count * (5 * n - 1)
    whole = pl.BlockSpec(memory_space=pltpu.VMEM)
    out_specs = [whole] * count
    if small is not None:
        operands += [small, *ready]
        depth, width = small.shape
        pieces = [pltpu.VMEM(s.shape, jnp.bfloat16) for s in out_shape]
        out_shape = [
            *[jax.ShapeDtypeStruct((8 * s.shape[0], s.shape[1]), s.dtype) for s in [*ready, *out_shape]],
            jax.ShapeDtypeStruct((depth, width // n), jnp.float32),
        ]
        out_specs = [pl.BlockSpec(memory_space=pltpu.HBM)] * (len(out_shape) - 1) + [whole]
        scratch = pieces + scratch + [
            pltpu.VMEM((depth, width), jnp.float32),
            pltpu.VMEM((3, depth, width), jnp.float32),
            pltpu.VMEM((n - 1, depth, width // n), jnp.float32),
            pltpu.SemaphoreType.DMA((len(ready) + count,)),
        ]
        copies += 3 + n - 1 + 8 * (len(ready) + count)
    return pl.pallas_call(
        partial(sums_kernel, n, plan, 0 if small is None else len(ready)),
        out_shape=out_shape,
        in_specs=[whole] * len(operands),
        out_specs=out_specs,
        scratch_shapes=[
            *scratch,
            pltpu.SemaphoreType.DMA((copies,)),
            pltpu.SemaphoreType.DMA((copies,)),
        ],
        compiler_params=pltpu.CompilerParams(
            collective_id=collective_id, has_side_effects=True, vmem_limit_bytes=63 * 1024 * 1024
        ),
        name="sum_products",
    )(*operands)


EARLY = (6, 7, 4, 5)
LATE = (2, 0, 1, 3)


def fallback_reduce(pairs):
    grad = jnp.concatenate([left_product(left, right) for left, right in pairs], axis=1)
    part = lax.psum_scatter(grad.astype(jnp.bfloat16), "fsdp", scatter_dimension=0, tiled=True)
    return lax.psum(part, "dp")


def on_device(
    fast,
    n,
    inputs,
    cotangent,
    lengths,
    buckets,
    ffn1_in,
    ffn1_out,
    attn_in,
    attn_out,
    conv_in,
    conv_out,
    ffn2_in,
    ffn2_out,
    norm_gains,
    pos_bias,
    kernel,
):
    shards = [ffn1_in, ffn1_out, attn_in, attn_out, conv_in, conv_out, ffn2_in, ffn2_out]
    width = norm_gains.shape[1]
    vectors = jnp.concatenate(
        [norm_gains, pos_bias, kernel, jnp.zeros((3, width), norm_gains.dtype)], axis=0
    )
    if fast:
        gathered = gather_all(n, shards, vectors, 0)
        weights, vec = gathered[:8], gathered[8]
        vec = vec.reshape(n, 16, width).transpose(1, 0, 2).reshape(16, D)
    else:
        weights = [lax.all_gather(s, "fsdp", axis=0, tiled=True) for s in shards]
        vec = lax.all_gather(vectors, "fsdp", axis=1, tiled=True)
    vec = vec.astype(jnp.float32)
    gains, biases, taps = vec[0:6], vec[6:8], vec[8:13]
    plans = [frame_plan(lengths[m], buckets[m]) for m in range(MICRO)]
    allowed = jnp.stack([p[0] for p in plans], axis=0).astype(jnp.float32)
    tap_masks = jnp.concatenate([p[1] for p in plans], axis=1)
    table_low = sinusoid(1).astype(jnp.bfloat16)
    mirror_low = sinusoid(-1).astype(jnp.bfloat16)

    stream = inputs.astype(jnp.float32)
    branch, kept_one = ffn_forward(stream, gains[0], weights[0], weights[1])
    section_one = stream + 0.5 * branch
    positions = matmul(table_low, weights[2][:, 3 * D :]).astype(jnp.bfloat16)
    mirrored = matmul(mirror_low, weights[2][:, 3 * D :]).astype(jnp.bfloat16)
    weight_qkv = weights[2][:, : 3 * D]
    branch, kept_two = attn_forward(
        section_one, gains[1], weight_qkv, weights[3], biases, positions, allowed
    )
    section_two = section_one + branch
    branch, kept_three = conv_forward(
        section_two, gains[2], gains[3], weights[4], weights[5], taps, tap_masks
    )
    section_three = section_two + branch
    branch, kept_four = ffn_forward(section_three, gains[4], weights[6], weights[7])
    section_four = section_three + 0.5 * branch
    final_out, final_pull = jax.vjp(layer_norm, section_four, gains[5])
    grad_stream, grad_final = final_pull(cotangent.astype(jnp.float32))

    grad_values, grad_vec4, grad_in4, grad_out4 = ffn_backward(
        0.5 * grad_stream, kept_four, weights[6], weights[7]
    )
    sums = [None] * 8
    grad_stream = grad_stream + grad_values
    grad_values, grad_vec3, grad_in3, grad_out3 = conv_backward(
        grad_stream, kept_three, weights[4], weights[5]
    )
    grad_stream = grad_stream + grad_values
    grad_values, grad_vec2, grad_in2, grad_out2, grad_pos = attn_backward(
        grad_stream, kept_two, weight_qkv, weights[3], biases, mirrored
    )
    grad_stream = grad_stream + grad_values
    grad_values, grad_vec1, grad_in1, grad_out1 = ffn_backward(
        0.5 * grad_stream, kept_one, weights[0], weights[1]
    )
    grad_in2 = grad_in2 + [(mirror_low, grad_pos)]
    grad_stream = grad_stream + grad_values

    grad_vectors = jnp.concatenate(
        [
            grad_vec1,
            grad_vec2[0:1],
            grad_vec3[0:2],
            grad_vec4,
            grad_final[None],
            grad_vec2[1:3],
            grad_vec3[2:7],
            jnp.zeros((3, D), jnp.float32),
        ],
        axis=0,
    )
    tensors = [grad_in1, grad_out1, grad_in2, grad_out2, grad_in3, grad_out3, grad_in4, grad_out4]
    if fast:
        early = sum_products(n, [tensors[i] for i in EARLY], None, (), 1)
        *wholes, grad_small = sum_products(n, [tensors[i] for i in LATE], grad_vectors, early, 2)
        for index, total in zip(EARLY + LATE, wholes):
            sums[index] = total
    else:
        sums = [fallback_reduce(pairs) for pairs in tensors]
        grad_small = lax.psum(
            lax.psum_scatter(grad_vectors, "fsdp", scatter_dimension=1, tiled=True), "dp"
        )
    grads = [s.astype(jnp.float32) for s in sums]
    return (
        final_out.astype(jnp.bfloat16),
        grad_stream,
        *grads,
        grad_small[0:6],
        grad_small[6:8],
        grad_small[8:13],
    )


def solution(mesh):
    in_specs = (
        P(("dp", "fsdp"), None),
        P(("dp", "fsdp"), None),
        P(("dp", "fsdp"), None),
        P(("dp", "fsdp")),
        P("fsdp", None),
        P("fsdp", None),
        P("fsdp", None),
        P("fsdp", None),
        P("fsdp", None),
        P("fsdp", None),
        P("fsdp", None),
        P("fsdp", None),
        P(None, "fsdp"),
        P(None, "fsdp"),
        P(None, "fsdp"),
    )
    out_specs = (
        P(("dp", "fsdp"), None),
        P(("dp", "fsdp"), None),
        P("fsdp", None),
        P("fsdp", None),
        P("fsdp", None),
        P("fsdp", None),
        P("fsdp", None),
        P("fsdp", None),
        P("fsdp", None),
        P("fsdp", None),
        P(None, "fsdp"),
        P(None, "fsdp"),
        P(None, "fsdp"),
    )
    sizes = dict(mesh.shape)
    n = sizes["fsdp"]
    fast = sizes["dp"] == 8 and n == 4
    return jax.shard_map(
        partial(on_device, fast, n), mesh=mesh, in_specs=in_specs, out_specs=out_specs, check_vma=False
    )
```
